256 devices in a mesh: grp: 8 (over x_lo, y), tile: 32 (over z, x_hi, core).
Axes of the slice: x: 4 (x_hi: 2, x_lo: 2; x = x_hi * 2 + x_lo), y: 4, z: 8, core: 2. Of those that a mesh axis runs over, the one named last changes fastest.
Arguments:
- pool_input: float32 [64, 2048, 256], P('grp', 'tile'), may hold values from 0 to 20
- weight_first: bfloat16 [3, 3, 256, 512], replicated, may hold values from -0.125 to 0.125
- weight_second: bfloat16 [3, 3, 512, 512], replicated, may hold values from -0.09375 to 0.09375
- targets: float32 [2, 512, 512], replicated, may hold values from -0.3 to 0.3
Outputs:
- image_grad: float32 [64, 2048, 256], P('grp', 'tile')
The draws below stay inside these ranges and needn't reach their ends.
All inputs are finite; a program needn't handle non-finite values.
Results may differ from the reference program's by a relative error of at most 0.0028.
Values may be sent and summed in bfloat16 or wider, within the bound.
A program may use at most 64 MiB of HBM per device.

```python
import jax
import jax.numpy as jnp
from jax import lax

C0 = 256
C1 = 512
H = 64
W = 2048


def draw_pool_input(key, part):
    key_rough = jax.random.fold_in(key, 11)
    key_base = jax.random.fold_in(key, 12)
    ramp = 0.6 + 1.2 * jnp.arange(W, dtype=jnp.float32) / W
    rough = jnp.exp(jax.random.uniform(key_rough, (H, W, 1), jnp.float32, -0.7, 0.7))
    base = jnp.abs(jax.random.normal(key_base, (H, W, C0), jnp.float32))
    return jnp.clip(base * ramp[None, :, None] * rough, 0.0, 20.0)


def gaussian(stream_key, dims, spread, limit, kind=jnp.bfloat16):
    entries = spread * jax.random.normal(stream_key, dims, jnp.float32)
    return jnp.clip(entries, min=-limit, max=limit).astype(kind)


def setup_inputs(seed: int = 0) -> dict:
    seeds = jax.random.split(jax.random.key(seed), 5)
    return {
        "pool_input": draw_pool_input(jax.random.fold_in(seeds[4], 71), 0),
        "weight_first": gaussian(seeds[1], (3, 3, C0, C1), (9 * C0) ** -0.5, 0.125),
        "weight_second": gaussian(seeds[2], (3, 3, C1, C1), (9 * C1) ** -0.5, 0.09375),
        "targets": gaussian(seeds[3], (2, C1, C1), 0.05, 0.3, jnp.float32),
    }


GELU_SCALE = 0.7978845608
GELU_CUBIC = 0.044715


def gelu_value(values):
    return 0.5 * values * (1.0 + jnp.tanh(GELU_SCALE * (values + GELU_CUBIC * values ** 3)))


def gelu_slope(values):
    hyper = jnp.tanh(GELU_SCALE * (values + GELU_CUBIC * values ** 3))
    return 0.5 * (1.0 + hyper) + 0.5 * values * (1.0 - hyper * hyper) * GELU_SCALE * (1.0 + 3.0 * GELU_CUBIC * values * values)


def conv_fwd(padded, weight, height, breadth):
    summed = None
    for row_shift in range(3):
        for col_shift in range(3):
            window = padded[row_shift:row_shift + height, col_shift:col_shift + breadth, :].reshape(height * breadth, -1)
            product = jnp.dot(window, weight[row_shift, col_shift], preferred_element_type=jnp.float32)
            summed = product if summed is None else summed + product
    return summed.reshape(height, breadth, -1)


def conv_back(padded, weight, height, breadth):
    summed = None
    for row_shift in range(3):
        for col_shift in range(3):
            window = padded[2 - row_shift:2 - row_shift + height, 2 - col_shift:2 - col_shift + breadth, :].reshape(height * breadth, -1)
            product = lax.dot_general(window, weight[row_shift, col_shift], (((1,), (1,)), ((), ())), preferred_element_type=jnp.float32)
            summed = product if summed is None else summed + product
    return summed.reshape(height, breadth, -1)


def pad_one(values):
    return jnp.pad(values, ((1, 1), (1, 1), (0, 0)))


def push_back(feature, target):
    positions = H * W
    flat = feature.reshape(positions, -1)
    centred = flat - jnp.sum(flat, axis=0) / positions
    gram_matrix = lax.dot_general(centred, centred, (((0,), (0,)), ((), ())), precision=lax.Precision.HIGHEST, preferred_element_type=jnp.float32) / positions
    mismatch = gram_matrix - target
    symmetric = (mismatch + mismatch.T) * 0.5
    return jnp.dot(centred, symmetric, precision=lax.Precision.HIGHEST, preferred_element_type=jnp.float32).reshape(H, W, -1)


def reference(pool_input, weight_first, weight_second, targets):
    pool_bf = pool_input.astype(jnp.bfloat16)
    pre_first = conv_fwd(pad_one(pool_bf), weight_first, H, W)
    act_first = gelu_value(pre_first)
    pre_second = conv_fwd(pad_one(act_first.astype(jnp.bfloat16)), weight_second, H, W)
    act_second = gelu_value(pre_second)
    push_first = push_back(act_first, targets[0])
    push_second = push_back(act_second, targets[1])
    grad_second = (push_second * gelu_slope(pre_second)).astype(jnp.bfloat16)
    flow_first = push_first + conv_back(pad_one(grad_second), weight_second, H, W)
    grad_first = (flow_first * gelu_slope(pre_first)).astype(jnp.bfloat16)
    return conv_back(pad_one(grad_first), weight_first, H, W)
```

```python
import functools

import jax
import jax.numpy as jnp
from jax import lax
from jax.experimental import pallas as pl
from jax.experimental.pallas import tpu as pltpu
from jax.sharding import PartitionSpec as P

GELU_SCALE = 0.7978845608
GELU_CUBIC = 0.044715
F32 = jnp.float32
BF16 = jnp.bfloat16
HIGHEST = lax.Precision.HIGHEST
MESH = pl.DeviceIdType.MESH
Z_TYPE = BF16
CELLS = 64 * 2048
OWN = 512
C0, C1 = 256, 512
W = 80


def gelu_value(z):
    return 0.5 * z * (1.0 + jnp.tanh(GELU_SCALE * (z + GELU_CUBIC * (z * z * z))))


def gelu_both(z):
    square = z * z
    hyper = jnp.tanh(GELU_SCALE * (z + GELU_CUBIC * (square * z)))
    half = 0.5 * (1.0 + hyper)
    slope = half + 0.5 * z * (1.0 - hyper * hyper) * GELU_SCALE * (1.0 + 3.0 * GELU_CUBIC * square)
    return z * half, slope


def flat(block):
    return block.reshape(block.shape[0] * block.shape[1], block.shape[2])


def dot_nn(left, right):
    return jnp.dot(left, right, preferred_element_type=F32)


def dot_nt(left, right):
    return lax.dot_general(left, right, (((1,), (1,)), ((), ())), preferred_element_type=F32)


def ahead(x, step):
    return x if step == 0 else pltpu.roll(x, (-step) % x.shape[0], 0)


def kernel(
    pool_hbm, w1_hbm, w2_hbm, tg_hbm, out,
    pool, w1, w2, tg, ts, pad, xs, pre1, act1, sl1, fsm, fs, act2m, act2, sl2,
    ch1, cl1, ch2, cl2, gs2, gs1, s0, r0, tsum, r1, means, dxs, zb, zm, ga, sh, sl, mean_ref,
    local_sem, halo_send, halo_recv, pair_send, pair_recv, rs_send, rs_recv,
    z_send, z_recv, ag_send, ag_recv, fw_send, fw_recv,
):
    g = lax.axis_index("grp")
    t = lax.axis_index("tile")
    core = lax.rem(t, 2)
    x_hi = lax.rem(t // 2, 2)
    z = t // 4
    k = x_hi * 8 + g
    strip = core * 16 + k

    partner = (g, z * 4 + x_hi * 2 + 1 - core)

    def xy_peer(other):
        return (lax.rem(other, 8), z * 4 + (other // 8) * 2 + core)

    def z_peer(other):
        return (g, other * 4 + x_hi * 2 + core)

    sides = [(i, j) for i in (-1, 0, 1) for j in (-1, 0, 1) if (i, j) != (0, 0)]

    def side_peer(i, j):
        return (lax.rem(g + i + 8, 8), lax.rem(t + j + 32, 32))

    loads = [
        pltpu.make_async_copy(source, target, local_sem.at[i])
        for i, (source, target) in enumerate(
            ((pool_hbm, pool), (tg_hbm, tg), (w1_hbm, w1), (w2_hbm, w2))
        )
    ]
    for load in loads:
        load.start()
    barrier = pltpu.get_barrier_semaphore()

    def greet(device):
        pl.semaphore_signal(barrier, inc=1, device_id=device, device_id_type=MESH)

    for i, j in sides:
        greet(side_peer(i, j))
    greet(partner)

    def greet_xy(i, carry):
        greet(xy_peer(lax.rem(k + i, 16)))
        return carry

    def greet_z(i, carry):
        greet(z_peer(lax.rem(z + i, 8)))
        return carry

    lax.fori_loop(1, 16, greet_xy, 0)
    lax.fori_loop(1, 8, greet_z, 0)
    loads[0].wait()
    pad[4:12, 16:80, :] = pool[...].astype(BF16)
    pl.semaphore_wait(barrier, 31)

    rows_from = {1: (8, 4), 0: (4, 8), -1: (4, 4)}
    rows_to = {1: (0, 4), 0: (4, 8), -1: (12, 4)}
    cols_from = {1: (64, 16), 0: (16, 64), -1: (16, 16)}
    cols_to = {1: (0, 16), 0: (16, 64), -1: (80, 16)}
    halos = []
    for n, (i, j) in enumerate(sides):
        (fr, nr), (fc, nc) = rows_from[i], cols_from[j]
        (tr, _), (tc, _) = rows_to[i], cols_to[j]
        halos.append(
            pltpu.make_async_remote_copy(
                src_ref=pad.at[pl.ds(fr, nr), pl.ds(fc, nc)],
                dst_ref=pad.at[pl.ds(tr, nr), pl.ds(tc, nc)],
                send_sem=halo_send.at[n],
                recv_sem=halo_recv.at[n],
                device_id=side_peer(i, j),
                device_id_type=MESH,
            )
        )
    for copy in halos:
        copy.start()

    loads[1].wait()
    for l in range(2):
        whole = tg[l]
        ts[l] = (whole + whole.T) * 0.5
    loads[2].wait()
    loads[3].wait()
    for copy in halos:
        copy.wait_recv()

    def clear_edges(ref, up, down, left, right):
        @pl.when(g == 0)
        def _():
            ref[0:up] = jnp.zeros((up, *ref.shape[1:]), ref.dtype)

        @pl.when(g == 7)
        def _():
            ref[ref.shape[0] - down :] = jnp.zeros((down, *ref.shape[1:]), ref.dtype)

        @pl.when(t == 0)
        def _():
            ref[:, 0:left] = jnp.zeros((ref.shape[0], left, ref.shape[2]), ref.dtype)

        @pl.when(t == 31)
        def _():
            ref[:, ref.shape[1] - right :] = jnp.zeros(
                (ref.shape[0], right, ref.shape[2]), ref.dtype
            )

    clear_edges(pad, 4, 4, 16, 16)

    def shift_pool(r, carry):
        x = pad[r].astype(F32)
        for b in range(3):
            xs[r, :, b * C0 : (b + 1) * C0] = ahead(x, b - 1)[8 : 8 + W].astype(BF16)
        return carry

    def conv1(first, rows):
        total = None
        for a in range(3):
            part = dot_nn(flat(xs[pl.ds(first + a, rows)]), w1[a])
            total = part if total is None else total + part
        pre1[pl.ds(first, rows)] = total.reshape(rows, W, C1)

    def gelu_row(r, carry):
        act1[r] = gelu_value(pre1[r])
        return carry

    lax.fori_loop(2, 14, shift_pool, 0)

    def conv1_step(i, carry):
        conv1(2 + 5 * i, 5)
        return carry

    lax.fori_loop(0, 2, conv1_step, 0)
    lax.fori_loop(2, 12, gelu_row, 0)
    clear_edges(act1.at[pl.ds(2, 10)], 1, 1, 8, 8)

    def shift_first(r, carry):
        x = act1[r + 2]
        for b in range(3):
            fsm[r, :, b * C1 : (b + 1) * C1] = ahead(x, b - 1)[8:72].astype(BF16)
        return carry

    lax.fori_loop(0, 10, shift_first, 0)

    def local_gram(l, x):
        mean = jnp.sum(x, axis=0, keepdims=True) * (1.0 / OWN)
        means[l, 2 * k + core] = mean
        cen = (x - mean).astype(BF16)
        gram = lax.dot_general(cen, cen, (((0,), (0,)), ((), ())), preferred_element_type=F32)
        for i in range(4):
            for d in range(3):
                j = (i + d) % 4
                block = gram[128 * i : 128 * i + 128, 128 * j : 128 * j + 128].astype(BF16)
                s0[l, i // 2, (i % 2) * 8 : (i % 2) * 8 + 8, :, 128 * d : 128 * d + 128] = (
                    block.reshape(8, 16, 128)
                )

    def pair_copies(l):
        return (
            pltpu.make_async_remote_copy(
                src_ref=s0.at[l, 1 - core],
                dst_ref=r0.at[l],
                send_sem=pair_send.at[l, 0],
                recv_sem=pair_recv.at[l, 0],
                device_id=partner,
                device_id_type=MESH,
            ),
            pltpu.make_async_remote_copy(
                src_ref=means.at[l, 2 * k + core],
                dst_ref=means.at[l, 2 * k + core],
                send_sem=pair_send.at[l, 1],
                recv_sem=pair_recv.at[l, 1],
                device_id=partner,
                device_id_type=MESH,
            ),
        )

    def rs_copies(l, to, slot):
        return (
            pltpu.make_async_remote_copy(
                src_ref=tsum.at[l, to],
                dst_ref=r1.at[l, slot],
                send_sem=rs_send.at[l, 0, to],
                recv_sem=rs_recv.at[l, 0, slot],
                device_id=xy_peer(to),
                device_id_type=MESH,
            ),
            pltpu.make_async_remote_copy(
                src_ref=means.at[l, pl.ds(2 * k, 2)],
                dst_ref=means.at[l, pl.ds(2 * slot, 2)],
                send_sem=rs_send.at[l, 1, to],
                recv_sem=rs_recv.at[l, 1, slot],
                device_id=xy_peer(to),
                device_id_type=MESH,
            ),
        )

    def pair_start(l):
        for copy in pair_copies(l):
            copy.start()

    def rs_start(l):
        for copy in pair_copies(l):
            copy.wait_recv()
        tsum[l] = (s0[l, core].astype(F32) + r0[l].astype(F32)).astype(BF16)
        r1[l, k] = tsum[l, k]

        def send(i, carry):
            for copy in rs_copies(l, lax.rem(k + i, 16), k):
                copy.start()
            return carry

        lax.fori_loop(1, 16, send, 0)

    def rs_wait(l):
        def wait(i, carry):
            other = lax.rem(k + 16 - i, 16)
            for copy in rs_copies(l, other, other):
                copy.wait_recv()
            return carry

        lax.fori_loop(1, 16, wait, 0)

    def spread(rows):
        mean = jnp.sum(rows, axis=0, keepdims=True) * (1.0 / rows.shape[0])
        off = rows - mean
        n = rows.shape[0]
        dxs[0:n, 0:C1] = off
        dxs[0:n, C1:] = off[:, 0:256]
        lane = lax.broadcasted_iota(jnp.int32, (16, C1), 1)
        sub = lax.broadcasted_iota(jnp.int32, (16, C1), 0)
        pick = jnp.where(lane == strip * 16 + sub, 1.0, 0.0).astype(F32)
        left = lax.dot_general(
            pick, off, (((1,), (1,)), ((), ())), precision=HIGHEST, preferred_element_type=F32
        )
        right = dxs[0:n, pl.ds(pl.multiple_of((strip // 8) * 128, 128), 384)]
        return mean, jnp.dot(left, right, precision=HIGHEST, preferred_element_type=F32)

    def z_copies(to, slot):
        return (
            pltpu.make_async_remote_copy(
                src_ref=zb.at[z],
                dst_ref=zb.at[slot],
                send_sem=z_send.at[0, to],
                recv_sem=z_recv.at[0, slot],
                device_id=z_peer(to),
                device_id_type=MESH,
            ),
            pltpu.make_async_remote_copy(
                src_ref=zm.at[z],
                dst_ref=zm.at[slot],
                send_sem=z_send.at[1, to],
                recv_sem=z_recv.at[1, slot],
                device_id=z_peer(to),
                device_id_type=MESH,
            ),
        )

    def ag_copy(to, slot):
        return pltpu.make_async_remote_copy(
            src_ref=ga.at[core, k],
            dst_ref=ga.at[core, slot],
            send_sem=ag_send.at[to],
            recv_sem=ag_recv.at[slot],
            device_id=xy_peer(to),
            device_id_type=MESH,
        )

    def fw_copy(side, slot):
        return pltpu.make_async_remote_copy(
            src_ref=ga.at[side, slot],
            dst_ref=ga.at[side, slot],
            send_sem=fw_send.at[slot],
            recv_sem=fw_recv.at[slot],
            device_id=partner,
            device_id_type=MESH,
        )

    local_gram(0, flat(act1[3:11, 8:72, :]))
    pair_start(0)

    def conv2_main(i, carry):
        total = None
        for a in range(3):
            part = dot_nn(flat(fsm[pl.ds(4 * i + a, 4)]), w2[a])
            total = part if total is None else total + part
        act2m[pl.ds(4 * i, 4)] = gelu_value(total).reshape(4, 64, C1)
        return carry

    lax.fori_loop(0, 1, conv2_main, 0)
    rs_start(0)
    lax.fori_loop(1, 2, conv2_main, 0)
    local_gram(1, flat(act2m[...]))
    pair_start(1)

    lax.fori_loop(0, 2, shift_pool, 0)
    lax.fori_loop(14, 16, shift_pool, 0)
    rs_start(1)

    def conv1_rim(i, carry):
        conv1(12 * i, 2)
        return carry

    lax.fori_loop(0, 2, conv1_rim, 0)

    def finish_first(r, carry):
        value, slope = gelu_both(pre1[r])
        act1[r] = value
        sl1[r] = slope
        return carry

    lax.fori_loop(0, 14, finish_first, 0)
    clear_edges(act1, 3, 3, 8, 8)
    clear_edges(sl1.at[pl.ds(2, 10)], 1, 1, 8, 8)

    def shift_first_all(r, carry):
        x = act1[r]
        for b in range(3):
            fs[r, :, b * C1 : (b + 1) * C1] = ahead(x, b - 1).astype(BF16)
        return carry

    lax.fori_loop(0, 14, shift_first_all, 0)

    rs_wait(0)
    rs_wait(1)
    for l in range(2):
        mean, extra = spread(means[l].reshape(32, C1))
        total = jnp.sum(r1[l].astype(F32), axis=0) + float(OWN) * extra
        zb[z, l] = total.astype(Z_TYPE)
        zm[z, l] = mean

    def z_send_step(i, carry):
        for copy in z_copies(lax.rem(z + i, 8), z):
            copy.start()
        return carry

    lax.fori_loop(1, 8, z_send_step, 0)

    def conv2_all(i, carry):
        total = None
        for a in range(3):
            part = dot_nn(flat(fs[pl.ds(4 * i + a, 4)]), w2[a])
            total = part if total is None else total + part
        value, slope = gelu_both(total)
        act2[pl.ds(4 * i, 4)] = value.reshape(4, W, C1)
        sl2[pl.ds(4 * i, 4)] = slope.reshape(4, W, C1)
        return carry

    lax.fori_loop(0, 2, conv2_all, 0)

    def z_wait_step(i, carry):
        other = lax.rem(z + 8 - i, 8)
        for copy in z_copies(other, other):
            copy.wait_recv()
        return carry

    lax.fori_loop(1, 8, z_wait_step, 0)
    for l in range(2):
        mean, extra = spread(zm[:, l].reshape(8, C1))
        total = jnp.sum(zb[:, l].astype(F32), axis=0) + float(32 * OWN) * extra
        mean_ref[l] = mean
        ga[core, k, l] = (total * (1.0 / CELLS)).astype(BF16)

    def ag_send_step(i, carry):
        ag_copy(lax.rem(k + i, 16), k).start()
        return carry

    lax.fori_loop(1, 16, ag_send_step, 0)
    fw_copy(core, k).start()

    lax.fori_loop(2, 3, conv2_all, 0)
    clear_edges(sl2, 2, 2, 8, 8)

    def ag_wait_step(i, carry):
        other = lax.rem(k + 16 - i, 16)
        ag_copy(other, other).wait_recv()
        fw_copy(core, other).start()
        return carry

    lax.fori_loop(1, 16, ag_wait_step, 0)

    def centre(source, high, low, mean, shift):
        def step(r, carry):
            cen = source[r + shift] - mean
            top = cen.astype(BF16)
            high[r] = top
            low[r] = (cen - top.astype(F32)).astype(BF16)
            return carry

        return step

    lax.fori_loop(0, 12, centre(act2, ch2, cl2, mean_ref[1], 0), 0)
    lax.fori_loop(0, 10, centre(act1, ch1, cl1, mean_ref[0], 2), 0)

    def fw_wait_step(slot, carry):
        fw_copy(1 - core, slot).wait_recv()
        return carry

    lax.fori_loop(0, 16, fw_wait_step, 0)

    def put(l, i, j, block):
        block = block - ts[l, 128 * i : 128 * i + 128, 128 * j : 128 * j + 128]
        top = block.astype(BF16)
        sh[l, 128 * i : 128 * i + 128, 128 * j : 128 * j + 128] = top
        sl[l, 128 * i : 128 * i + 128, 128 * j : 128 * j + 128] = (
            block - top.astype(F32)
        ).astype(BF16)

    for l in (1, 0):
        for i in range(4):
            strips = ga[i // 2, (i % 2) * 8 : (i % 2) * 8 + 8, l].astype(F32).reshape(128, 384)
            for d in range(3):
                block = strips[:, 128 * d : 128 * d + 128]
                put(l, i, (i + d) % 4, block)
                if d == 1:
                    put(l, (i + 1) % 4, i, block.T)

    def push(l, high, low, first, rows):
        top = flat(high[pl.ds(first, rows)])
        rest = flat(low[pl.ds(first, rows)])
        return dot_nn(top, sh[l]) + dot_nn(rest, sh[l]) + dot_nn(top, sl[l])

    def back2(i, carry):
        grad = push(1, ch2, cl2, 4 * i, 4) * flat(sl2[pl.ds(4 * i, 4)])
        for b in range(3):
            gs2[pl.ds(4 * i, 4), :, b * C1 : (b + 1) * C1] = (
                ahead(grad, 1 - b).astype(BF16).reshape(4, W, C1)
            )
        return carry

    lax.fori_loop(0, 3, back2, 0)

    def back1(i, carry):
        flow = push(0, ch1, cl1, 5 * i, 5)
        for a in range(3):
            for b in range(3):
                flow = flow + dot_nt(
                    flat(gs2[pl.ds(5 * i + 2 - a, 5), :, b * C1 : (b + 1) * C1]),
                    w2[a, b * C1 : (b + 1) * C1, :],
                )
        grad = flow * flat(sl1[pl.ds(5 * i + 2, 5)])
        for b in range(3):
            gs1[pl.ds(5 * i, 5), :, b * C1 : (b + 1) * C1] = (
                ahead(grad, 1 - b).reshape(5, W, C1)[:, 8:72].astype(BF16)
            )
        return carry

    lax.fori_loop(0, 2, back1, 0)

    def back0(i, carry):
        total = None
        for a in range(3):
            for b in range(3):
                part = dot_nt(
                    flat(gs1[pl.ds(4 * i + 2 - a, 4), :, b * C1 : (b + 1) * C1]),
                    w1[a, b * C0 : (b + 1) * C0, :],
                )
                total = part if total is None else total + part
        out[pl.ds(4 * i, 4)] = total.reshape(4, 64, C0)
        return carry

    lax.fori_loop(0, 2, back0, 0)

    for copy in halos:
        copy.wait_send()
    for l in range(2):
        for copy in pair_copies(l):
            copy.wait_send()

    def rs_drain(i, carry):
        for l in range(2):
            for copy in rs_copies(l, lax.rem(k + i, 16), k):
                copy.wait_send()
        ag_copy(lax.rem(k + i, 16), k).wait_send()
        return carry

    lax.fori_loop(1, 16, rs_drain, 0)

    def z_drain(i, carry):
        for copy in z_copies(lax.rem(z + i, 8), z):
            copy.wait_send()
        return carry

    lax.fori_loop(1, 8, z_drain, 0)

    def fw_drain(slot, carry):
        fw_copy(core, slot).wait_send()
        return carry

    lax.fori_loop(0, 16, fw_drain, 0)


def local(pool_input, weight_first, weight_second, targets):
    v = pltpu.VMEM
    dma = pltpu.SemaphoreType.DMA
    scratch = [
        v((8, 64, C0), F32),
        v((3, 3 * C0, C1), BF16),
        v((3, 3 * C1, C1), BF16),
        v((2, C1, C1), F32),
        v((2, C1, C1), F32),
        v((16, 96, C0), BF16),
        v((16, W, 3 * C0), BF16),
        v((14, W, C1), F32),
        v((14, W, C1), F32),
        v((14, W, C1), F32),
        v((10, 64, 3 * C1), BF16),
        v((14, W, 3 * C1), BF16),
        v((8, 64, C1), F32),
        v((12, W, C1), F32),
        v((12, W, C1), F32),
        v((10, W, C1), BF16),
        v((10, W, C1), BF16),
        v((12, W, C1), BF16),
        v((12, W, C1), BF16),
        v((12, W, 3 * C1), BF16),
        v((10, 64, 3 * C1), BF16),
        v((2, 2, 16, 16, 384), BF16),
        v((2, 16, 16, 384), BF16),
        v((2, 16, 16, 384), BF16),
        v((2, 16, 16, 384), BF16),
        v((2, 32, 1, C1), F32),
        v((32, C1 + 256), F32),
        v((8, 2, 16, 384), Z_TYPE),
        v((8, 2, 1, C1), F32),
        v((2, 16, 2, 16, 384), BF16),
        v((2, C1, C1), BF16),
        v((2, C1, C1), BF16),
        v((2, 1, C1), F32),
        dma((4,)),
        dma((8,)),
        dma((8,)),
        dma((2, 2)),
        dma((2, 2)),
        dma((2, 2, 16)),
        dma((2, 2, 16)),
        dma((2, 8)),
        dma((2, 8)),
        dma((16,)),
        dma((16,)),
        dma((16,)),
        dma((16,)),
    ]
    anywhere = pl.BlockSpec(memory_space=pl.ANY)
    return pl.pallas_call(
        kernel,
        out_shape=jax.ShapeDtypeStruct((8, 64, C0), F32),
        in_specs=[anywhere] * 4,
        out_specs=pl.BlockSpec(memory_space=pltpu.VMEM),
        scratch_shapes=scratch,
        compiler_params=pltpu.CompilerParams(
            collective_id=0, has_side_effects=True, vmem_limit_bytes=67043328
        ),
        name="style_grad",
    )(
        pool_input,
        weight_first.reshape(3, 3 * C0, C1),
        weight_second.reshape(3, 3 * C1, C1),
        targets,
    )


def solution(mesh):
    return jax.shard_map(
        local,
        mesh=mesh,
        in_specs=(P("grp", "tile", None), P(), P(), P()),
        out_specs=P("grp", "tile", None),
        check_vma=False,
    )
```

```python
import functools

import jax
import jax.numpy as jnp
from jax import lax
from jax.experimental import pallas as pl
from jax.experimental.pallas import tpu as pltpu
from jax.sharding import PartitionSpec as P

GELU_SCALE = 0.7978845608
GELU_CUBIC = 0.044715
F32 = jnp.float32
BF16 = jnp.bfloat16
HIGHEST = lax.Precision.HIGHEST
MESH = pl.DeviceIdType.MESH
Z_TYPE = BF16
CELLS = 64 * 2048
OWN = 512
C0, C1 = 256, 512
W = 80


def gelu_value(z):
    return 0.5 * z * (1.0 + jnp.tanh(GELU_SCALE * (z + GELU_CUBIC * (z * z * z))))


def gelu_both(z):
    square = z * z
    hyper = jnp.tanh(GELU_SCALE * (z + GELU_CUBIC * (square * z)))
    half = 0.5 * (1.0 + hyper)
    slope = half + 0.5 * z * (1.0 - hyper * hyper) * GELU_SCALE * (1.0 + 3.0 * GELU_CUBIC * square)
    return z * half, slope


def flat(block):
    return block.reshape(block.shape[0] * block.shape[1], block.shape[2])


def dot_nn(left, right):
    return jnp.dot(left, right, preferred_element_type=F32)


def dot_nt(left, right):
    return lax.dot_general(left, right, (((1,), (1,)), ((), ())), preferred_element_type=F32)


def ahead(x, step):
    return x if step == 0 else pltpu.roll(x, (-step) % x.shape[0], 0)


def kernel(
    pool_hbm, w1_hbm, w2_hbm, tg_hbm, out_hbm,
    pool, w1, w2, tg, ts, pad, xs, pre1, act1, sl1, fsm, fs, act2m, act2, sl2,
    ch1, cl1, ch2, cl2, s0, r0, tsum, r1, means, dxs, zb, zm, ga, sh, sl, outv,
    local_sem, halo_send, halo_recv, pair_send, pair_recv, rs_send, rs_recv,
    z_send, z_recv, ag_send, ag_recv, fw_send, fw_recv,
):
    gs1, gs2, flow1 = fsm, fs, pre1
    g = lax.axis_index("grp")
    t = lax.axis_index("tile")
    core = lax.rem(t, 2)
    x = lax.rem(t // 2, 2) * 2 + g // 4
    y = lax.rem(g, 4)
    z = t // 4
    k = x * 4 + y
    strip = core * 16 + k

    def device(x_to, y_to, z_to, core_to):
        return (lax.rem(x_to, 2) * 4 + y_to, z_to * 4 + (x_to // 2) * 2 + core_to)

    partner = device(x, y, z, 1 - core)

    def xy_peer(other):
        return device(other // 4, lax.rem(other, 4), z, core)

    def z_peer(other):
        return device(x, y, other, core)

    xy_steps = sorted(
        ((i, j) for i in range(4) for j in range(4) if (i, j) != (0, 0)),
        key=lambda s: -(min(s[0], 4 - s[0]) + min(s[1], 4 - s[1])),
    )
    xy_others = [lax.rem(x + i, 4) * 4 + lax.rem(y + j, 4) for i, j in xy_steps]
    z_others = [lax.rem(z + i, 8) for i in (4, 3, 5, 2, 6, 1, 7)]
    sides = [(i, j) for i in (-1, 1) for j in (-1, 1, 0)] + [(0, -1), (0, 1)]

    def side_peer(i, j):
        return (lax.rem(g + i + 8, 8), lax.rem(t + j + 32, 32))

    loads = [
        pltpu.make_async_copy(source, target, local_sem.at[i])
        for i, (source, target) in enumerate(
            ((pool_hbm, pool), (tg_hbm, tg), (w1_hbm, w1), (w2_hbm, w2))
        )
    ]
    for load in loads:
        load.start()
    barrier = pltpu.get_barrier_semaphore()

    def greet(who):
        pl.semaphore_signal(barrier, inc=1, device_id=who, device_id_type=MESH)

    for i, j in sides:
        greet(side_peer(i, j))
    for other in xy_others:
        greet(xy_peer(other))
    for other in z_others:
        greet(z_peer(other))
    greet(partner)
    loads[0].wait()
    pad[4:12, 1:9] = pool[...].astype(BF16).reshape(8, 8, 8, C0)
    pl.semaphore_wait(barrier, 31)

    cols_from = {1: (8, 1), 0: (1, 8), -1: (1, 1)}
    cols_to = {1: (0, 1), 0: (1, 8), -1: (9, 1)}

    def halo(n, i, j, row_from, row_to, rows):
        (fc, nc), (tc, _) = cols_from[j], cols_to[j]
        return pltpu.make_async_remote_copy(
            src_ref=pad.at[pl.ds(row_from, rows), pl.ds(fc, nc)],
            dst_ref=pad.at[pl.ds(row_to, rows), pl.ds(tc, nc)],
            send_sem=halo_send.at[n],
            recv_sem=halo_recv.at[n],
            device_id=side_peer(i, j),
            device_id_type=MESH,
        )

    near_rows = {1: (10, 2, 2), 0: (4, 4, 8), -1: (4, 12, 2)}
    far_rows = {1: (8, 0, 2), -1: (6, 14, 2)}
    near = [halo(n, i, j, *near_rows[i]) for n, (i, j) in enumerate(sides)]
    far = [halo(8 + n, i, j, *far_rows[i]) for n, (i, j) in enumerate(sides) if i != 0]
    for copy in near + far:
        copy.start()

    loads[1].wait()
    for l in range(2):
        whole = tg[l]
        ts[l] = (whole + whole.T) * 0.5
    loads[2].wait()
    loads[3].wait()
    for copy in near:
        copy.wait_recv()

    def on_edges(top, bottom, left, right):
        pl.when(g == 0)(top)
        pl.when(g == 7)(bottom)
        pl.when(t == 0)(left)
        pl.when(t == 31)(right)

    def clear_pad(up, down, blocks):
        def zero(first, rows, col, cols):
            pad[first : first + rows, col : col + cols] = jnp.zeros((rows, cols, 8, C0), BF16)

        def column(col):
            for first, rows in blocks:
                zero(first, rows, col, 1)

        on_edges(
            lambda: zero(up, 2, 0, 10),
            lambda: zero(down, 2, 0, 10),
            lambda: column(0),
            lambda: column(9),
        )

    def clear_edges(ref, first, rows, depth):
        def zero(row, n, col, cols):
            ref[row : row + n, col : col + cols] = jnp.zeros((n, cols, ref.shape[2]), ref.dtype)

        on_edges(
            lambda: zero(first, depth, 0, W),
            lambda: zero(first + rows - depth, depth, 0, W),
            lambda: zero(first, rows, 0, 8),
            lambda: zero(first, rows, W - 8, 8),
        )

    clear_pad(2, 12, ((2, 12),))

    def shift_pool(r, carry):
        row = pad[r].astype(F32).reshape(W, C0)
        for b in range(3):
            xs[r, :, b * C0 : (b + 1) * C0] = ahead(row, b - 1).astype(BF16)
        return carry

    def conv1(first, rows):
        total = None
        for a in range(3):
            part = dot_nn(flat(xs[pl.ds(first + a, rows)]), w1[a])
            total = part if total is None else total + part
        pre1[pl.ds(first, rows)] = total.reshape(rows, W, C1)

    def gelu_row(r, carry):
        act1[r] = gelu_value(pre1[r])
        return carry

    lax.fori_loop(2, 14, shift_pool, 0)

    def conv1_step(i, carry):
        conv1(2 + 5 * i, 5)
        return carry

    lax.fori_loop(0, 2, conv1_step, 0)
    lax.fori_loop(2, 12, gelu_row, 0)
    clear_edges(act1, 2, 10, 1)

    def shift_first(r, carry):
        row = act1[r + 2]
        for b in range(3):
            fsm[r, :, b * C1 : (b + 1) * C1] = ahead(row, b - 1)[8:72].astype(BF16)
        return carry

    lax.fori_loop(0, 10, shift_first, 0)

    def remote(source, target, send, recv, who):
        return pltpu.make_async_remote_copy(
            src_ref=source, dst_ref=target, send_sem=send, recv_sem=recv,
            device_id=who, device_id_type=MESH,
        )

    def pair_piece(l):
        return remote(
            s0.at[l, 1 - core], r0.at[l], pair_send.at[l, 0], pair_recv.at[l, 0], partner
        )

    def pair_mean(l):
        own = means.at[l, 2 * k + core]
        return remote(own, own, pair_send.at[l, 1], pair_recv.at[l, 1], partner)

    def pair_mean_in(l):
        other = means.at[l, 2 * k + 1 - core]
        return remote(other, other, pair_send.at[l, 1], pair_recv.at[l, 1], partner)

    def rs_piece(l, to, slot):
        return remote(
            tsum.at[l, to], r1.at[l, slot], rs_send.at[l, 0, to], rs_recv.at[l, 0, slot], xy_peer(to)
        )

    def rs_mean(l, to, slot):
        both = means.at[l, pl.ds(2 * slot, 2)]
        return remote(both, both, rs_send.at[l, 1, to], rs_recv.at[l, 1, slot], xy_peer(to))

    def z_piece(l, to, slot):
        part = zb.at[l, slot]
        return remote(part, part, z_send.at[l, 0, to], z_recv.at[l, 0, slot], z_peer(to))

    def z_mean(l, to, slot):
        part = zm.at[l, slot]
        return remote(part, part, z_send.at[l, 1, to], z_recv.at[l, 1, slot], z_peer(to))

    def ag_piece(l, to, slot):
        part = ga.at[l, core, slot]
        return remote(part, part, ag_send.at[l, to], ag_recv.at[l, slot], xy_peer(to))

    def fw_piece(l, side, slot):
        part = ga.at[l, side, slot]
        return remote(part, part, fw_send.at[l, slot], fw_recv.at[l, slot], partner)

    def xy_wait(make, l):
        def step(i, carry):
            other = lax.rem(k + 16 - i, 16)
            make(l, other, other).wait_recv()
            return carry

        lax.fori_loop(1, 16, step, 0)

    def z_wait(make, l):
        def step(i, carry):
            other = lax.rem(z + 8 - i, 8)
            make(l, other, other).wait_recv()
            return carry

        lax.fori_loop(1, 8, step, 0)

    def local_gram(l, values):
        mean = jnp.sum(values, axis=0, keepdims=True) * (1.0 / OWN)
        means[l, 2 * k + core] = mean
        cen = (values - mean).astype(BF16)
        pair_mean(l).start()
        gram = lax.dot_general(cen, cen, (((0,), (0,)), ((), ())), preferred_element_type=F32)
        for i in range(4):
            for d in range(3):
                j = (i + d) % 4
                block = gram[128 * i : 128 * i + 128, 128 * j : 128 * j + 128].astype(BF16)
                s0[l, i // 2, (i % 2) * 8 : (i % 2) * 8 + 8, :, 128 * d : 128 * d + 128] = (
                    block.reshape(8, 16, 128)
                )
        pair_piece(l).start()

    def rs_start(l):
        pair_mean_in(l).wait_recv()
        for other in xy_others:
            rs_mean(l, other, k).start()
        pair_piece(l).wait_recv()
        tsum[l] = (s0[l, core].astype(F32) + r0[l].astype(F32)).astype(BF16)
        r1[l, k] = tsum[l, k]
        for other in xy_others:
            rs_piece(l, other, k).start()

    def spread(rows):
        n = rows.shape[0]
        mean = jnp.sum(rows, axis=0, keepdims=True) * (1.0 / n)
        off = rows - mean
        dxs[0:n, 0:C1] = off
        dxs[0:n, C1:] = off[:, 0:256]
        lane = lax.broadcasted_iota(jnp.int32, (16, C1), 1)
        sub = lax.broadcasted_iota(jnp.int32, (16, C1), 0)
        pick = jnp.where(lane == strip * 16 + sub, 1.0, 0.0).astype(F32)
        left = lax.dot_general(
            pick, off, (((1,), (1,)), ((), ())), precision=HIGHEST, preferred_element_type=F32
        )
        right = dxs[0:n, pl.ds(pl.multiple_of((strip // 8) * 128, 128), 384)]
        return mean, jnp.dot(left, right, precision=HIGHEST, preferred_element_type=F32)

    def plane_done(l):
        xy_wait(rs_mean, l)
        mean, extra = spread(means[l].reshape(32, C1))
        zm[l, z] = mean
        xy_wait(rs_piece, l)
        total = jnp.sum(r1[l].astype(F32), axis=0) + float(OWN) * extra
        zb[l, z] = total.astype(Z_TYPE)
        for other in z_others:
            z_mean(l, other, z).start()
        for other in z_others:
            z_piece(l, other, z).start()

    def z_done(l):
        z_wait(z_mean, l)
        mean, extra = spread(zm[l].reshape(8, C1))
        z_wait(z_piece, l)
        total = jnp.sum(zb[l].astype(F32), axis=0) + float(32 * OWN) * extra
        ga[l, core, k] = (total * (1.0 / CELLS)).astype(BF16)
        for other in xy_others:
            ag_piece(l, other, k).start()
        fw_piece(l, core, k).start()
        return mean

    def gathered(l):
        def step(i, carry):
            other = lax.rem(k + 16 - i, 16)
            ag_piece(l, other, other).wait_recv()
            fw_piece(l, core, other).start()
            return carry

        lax.fori_loop(1, 16, step, 0)

    def forwarded(l):
        def step(slot, carry):
            fw_piece(l, 1 - core, slot).wait_recv()
            return carry

        lax.fori_loop(0, 16, step, 0)

    def mismatch(l):
        def put(i, j, block):
            block = block - ts[l, 128 * i : 128 * i + 128, 128 * j : 128 * j + 128]
            top = block.astype(BF16)
            sh[l, 128 * i : 128 * i + 128, 128 * j : 128 * j + 128] = top
            sl[l, 128 * i : 128 * i + 128, 128 * j : 128 * j + 128] = (
                block - top.astype(F32)
            ).astype(BF16)

        for i in range(4):
            rows = ga[l, i // 2, (i % 2) * 8 : (i % 2) * 8 + 8].astype(F32).reshape(128, 384)
            for d in range(3):
                block = rows[:, 128 * d : 128 * d + 128]
                put(i, (i + d) % 4, block)
                if d == 1:
                    put((i + 1) % 4, i, block.T)

    local_gram(0, flat(act1[3:11, 8:72, :]))

    def conv2_main(i, carry):
        total = None
        for a in range(3):
            part = dot_nn(flat(fsm[pl.ds(4 * i + a, 4)]), w2[a])
            total = part if total is None else total + part
        act2m[pl.ds(4 * i, 4)] = gelu_value(total).reshape(4, 64, C1)
        return carry

    lax.fori_loop(0, 1, conv2_main, 0)
    rs_start(0)
    lax.fori_loop(1, 2, conv2_main, 0)
    local_gram(1, flat(act2m[...]))

    for copy in far:
        copy.wait_recv()
    clear_pad(0, 14, ((0, 2), (14, 2)))
    lax.fori_loop(0, 2, shift_pool, 0)
    lax.fori_loop(14, 16, shift_pool, 0)

    def conv1_rim(i, carry):
        conv1(12 * i, 2)
        return carry

    lax.fori_loop(0, 2, conv1_rim, 0)
    rs_start(1)

    plane_done(0)

    def finish_first(r, carry):
        value, slope = gelu_both(pre1[r])
        act1[r] = value
        sl1[r] = slope
        return carry

    lax.fori_loop(0, 14, finish_first, 0)
    clear_edges(act1, 0, 14, 3)
    clear_edges(sl1, 2, 10, 1)

    def shift_first_all(r, carry):
        row = act1[r]
        for b in range(3):
            fs[r, :, b * C1 : (b + 1) * C1] = ahead(row, b - 1).astype(BF16)
        return carry

    lax.fori_loop(0, 14, shift_first_all, 0)

    plane_done(1)

    def conv2_all(i, carry):
        total = None
        for a in range(3):
            part = dot_nn(flat(fs[pl.ds(4 * i + a, 4)]), w2[a])
            total = part if total is None else total + part
        value, slope = gelu_both(total)
        act2[pl.ds(4 * i, 4)] = value.reshape(4, W, C1)
        sl2[pl.ds(4 * i, 4)] = slope.reshape(4, W, C1)
        return carry

    lax.fori_loop(0, 1, conv2_all, 0)
    mean_first = z_done(0)
    lax.fori_loop(1, 2, conv2_all, 0)
    mean_second = z_done(1)
    lax.fori_loop(2, 3, conv2_all, 0)
    clear_edges(sl2, 0, 12, 2)

    def centre(source, high, low, mean, shift):
        def step(r, carry):
            cen = source[r + shift] - mean
            top = cen.astype(BF16)
            high[r] = top
            low[r] = (cen - top.astype(F32)).astype(BF16)
            return carry

        return step

    lax.fori_loop(0, 10, centre(act1, ch1, cl1, mean_first, 2), 0)
    lax.fori_loop(0, 12, centre(act2, ch2, cl2, mean_second, 0), 0)

    def push(l, high, low, first, rows):
        top = flat(high[pl.ds(first, rows)])
        rest = flat(low[pl.ds(first, rows)])
        return dot_nn(top, sh[l]) + dot_nn(rest, sh[l]) + dot_nn(top, sl[l])

    gathered(0)
    forwarded(0)
    mismatch(0)

    def push_first(i, carry):
        flow1[pl.ds(5 * i, 5)] = push(0, ch1, cl1, 5 * i, 5).reshape(5, W, C1)
        return carry

    lax.fori_loop(0, 2, push_first, 0)

    gathered(1)

    for copy in near + far:
        copy.wait_send()
    for l in range(2):
        pair_piece(l).wait_send()
        pair_mean(l).wait_send()

    def rs_drain(i, carry):
        for l in range(2):
            rs_piece(l, lax.rem(k + i, 16), k).wait_send()
            rs_mean(l, lax.rem(k + i, 16), k).wait_send()
        return carry

    lax.fori_loop(1, 16, rs_drain, 0)

    def z_drain(i, carry):
        for l in range(2):
            z_piece(l, lax.rem(z + i, 8), z).wait_send()
            z_mean(l, lax.rem(z + i, 8), z).wait_send()
        return carry

    lax.fori_loop(1, 8, z_drain, 0)
    forwarded(1)

    mismatch(1)

    def back2(i, carry):
        grad = push(1, ch2, cl2, 4 * i, 4) * flat(sl2[pl.ds(4 * i, 4)])
        for b in range(3):
            gs2[pl.ds(4 * i, 4), :, b * C1 : (b + 1) * C1] = (
                ahead(grad, 1 - b).astype(BF16).reshape(4, W, C1)
            )
        return carry

    lax.fori_loop(0, 3, back2, 0)

    def back1(i, carry):
        flow = flat(flow1[pl.ds(5 * i, 5)])
        for a in range(3):
            for b in range(3):
                flow = flow + dot_nt(
                    flat(gs2[pl.ds(5 * i + 2 - a, 5), :, b * C1 : (b + 1) * C1]),
                    w2[a, b * C1 : (b + 1) * C1, :],
                )
        grad = flow * flat(sl1[pl.ds(5 * i + 2, 5)])
        for b in range(3):
            gs1[pl.ds(5 * i, 5), :, b * C1 : (b + 1) * C1] = (
                ahead(grad, 1 - b).reshape(5, W, C1)[:, 8:72].astype(BF16)
            )
        return carry

    lax.fori_loop(0, 2, back1, 0)

    def out_copy(i):
        rows = pl.ds(4 * i, 4)
        return pltpu.make_async_copy(outv.at[rows], out_hbm.at[rows], local_sem.at[i])

    def back0(i, carry):
        total = None
        for a in range(3):
            for b in range(3):
                part = dot_nt(
                    flat(gs1[pl.ds(4 * i + 2 - a, 4), :, b * C1 : (b + 1) * C1]),
                    w1[a, b * C0 : (b + 1) * C0, :],
                )
                total = part if total is None else total + part
        outv[pl.ds(4 * i, 4)] = total.reshape(4, 64, C0)
        out_copy(i).start()
        return carry

    lax.fori_loop(0, 2, back0, 0)

    def ag_drain(i, carry):
        for l in range(2):
            ag_piece(l, lax.rem(k + i, 16), k).wait_send()
        return carry

    lax.fori_loop(1, 16, ag_drain, 0)

    def fw_drain(slot, carry):
        for l in range(2):
            fw_piece(l, core, slot).wait_send()
        return carry

    lax.fori_loop(0, 16, fw_drain, 0)
    for i in range(2):
        out_copy(i).wait()


def local(pool_input, weight_first, weight_second, targets):
    v = pltpu.VMEM
    dma = pltpu.SemaphoreType.DMA
    scratch = [
        v((8, 64, C0), F32),
        v((3, 3 * C0, C1), BF16),
        v((3, 3 * C1, C1), BF16),
        v((2, C1, C1), F32),
        v((2, C1, C1), F32),
        v((16, 10, 8, C0), BF16),
        v((16, W, 3 * C0), BF16),
        v((14, W, C1), F32),
        v((14, W, C1), F32),
        v((14, W, C1), F32),
        v((10, 64, 3 * C1), BF16),
        v((14, W, 3 * C1), BF16),
        v((8, 64, C1), F32),
        v((12, W, C1), F32),
        v((12, W, C1), F32),
        v((10, W, C1), BF16),
        v((10, W, C1), BF16),
        v((12, W, C1), BF16),
        v((12, W, C1), BF16),
        v((2, 2, 16, 16, 384), BF16),
        v((2, 16, 16, 384), BF16),
        v((2, 16, 16, 384), BF16),
        v((2, 16, 16, 384), BF16),
        v((2, 32, 1, C1), F32),
        v((32, C1 + 256), F32),
        v((2, 8, 16, 384), Z_TYPE),
        v((2, 8, 1, C1), F32),
        v((2, 2, 16, 16, 384), BF16),
        v((2, C1, C1), BF16),
        v((2, C1, C1), BF16),
        v((8, 64, C0), F32),
        dma((4,)),
        dma((16,)),
        dma((16,)),
        dma((2, 2)),
        dma((2, 2)),
        dma((2, 2, 16)),
        dma((2, 2, 16)),
        dma((2, 2, 8)),
        dma((2, 2, 8)),
        dma((2, 16)),
        dma((2, 16)),
        dma((2, 16)),
        dma((2, 16)),
    ]
    anywhere = pl.BlockSpec(memory_space=pl.ANY)
    return pl.pallas_call(
        kernel,
        out_shape=jax.ShapeDtypeStruct((8, 64, C0), F32),
        in_specs=[pl.BlockSpec(memory_space=pltpu.HBM)] * 4,
        out_specs=anywhere,
        scratch_shapes=scratch,
        compiler_params=pltpu.CompilerParams(
            collective_id=0, has_side_effects=True, vmem_limit_bytes=56 * 1024 * 1024
        ),
        name="style_grad",
    )(
        pool_input,
        weight_first.reshape(3, 3 * C0, C1),
        weight_second.reshape(3, 3 * C1, C1),
        targets,
    )


def solution(mesh):
    return jax.shard_map(
        local,
        mesh=mesh,
        in_specs=(P("grp", "tile", None), P(), P(), P()),
        out_specs=P("grp", "tile", None),
        check_vma=False,
    )
```

```python
import functools

import jax
import jax.numpy as jnp
from jax import lax
from jax.experimental import pallas as pl
from jax.experimental.pallas import tpu as pltpu
from jax.sharding import PartitionSpec as P

GELU_SCALE = 0.7978845608
GELU_CUBIC = 0.044715
F32 = jnp.float32
BF16 = jnp.bfloat16
HIGHEST = lax.Precision.HIGHEST
MESH = pl.DeviceIdType.MESH
Z_TYPE = BF16
CELLS = 64 * 2048
OWN = 512
C0, C1 = 256, 512
W = 80


def gelu_value(z):
    return 0.5 * z * (1.0 + jnp.tanh(GELU_SCALE * (z + GELU_CUBIC * (z * z * z))))


def gelu_both(z):
    square = z * z
    hyper = jnp.tanh(GELU_SCALE * (z + GELU_CUBIC * (square * z)))
    half = 0.5 * (1.0 + hyper)
    slope = half + 0.5 * z * (1.0 - hyper * hyper) * GELU_SCALE * (1.0 + 3.0 * GELU_CUBIC * square)
    return z * half, slope


def flat(block):
    return block.reshape(block.shape[0] * block.shape[1], block.shape[2])


def dot_nn(left, right):
    return jnp.dot(left, right, preferred_element_type=F32)


def dot_nt(left, right):
    return lax.dot_general(left, right, (((1,), (1,)), ((), ())), preferred_element_type=F32)


def ahead(x, step):
    return x if step == 0 else pltpu.roll(x, (-step) % x.shape[0], 0)


def kernel(
    pool_hbm, w1_hbm, w2_hbm, tg_hbm, out,
    pool, w1, w2, tg, ts, pad, xs, pre1, act1, sl1, fsm, fs, act2m, act2, sl2,
    ch1, cl1, ch2, cl2, s0, r0, tsum, r1, means, dxs, zb, zm, ga, sh, sl,
    local_sem, halo_sem, pair_send, pair_recv, rs_sem, z_sem, ag_send, ag_recv, fw_sem,
):
    gs1, gs2, flow1 = fsm, fs, pre1
    g = lax.axis_index("grp")
    t = lax.axis_index("tile")
    core = lax.rem(t, 2)
    x = lax.rem(t // 2, 2) * 2 + g // 4
    y = lax.rem(g, 4)
    z = t // 4
    k = x * 4 + y
    strip = core * 16 + k

    def device(x_to, y_to, z_to, core_to):
        return (lax.rem(x_to, 2) * 4 + y_to, z_to * 4 + (x_to // 2) * 2 + core_to)

    partner = device(x, y, z, 1 - core)

    def xy_peer(other):
        return device(other // 4, lax.rem(other, 4), z, core)

    def z_peer(other):
        return device(x, y, other, core)

    xy_steps = sorted(
        ((i, j) for i in range(4) for j in range(4) if (i, j) != (0, 0)),
        key=lambda s: -(min(s[0], 4 - s[0]) + min(s[1], 4 - s[1])),
    )
    xy_others = [lax.rem(x + i, 4) * 4 + lax.rem(y + j, 4) for i, j in xy_steps]
    xy_from = [lax.rem(x + 4 - i, 4) * 4 + lax.rem(y + 4 - j, 4) for i, j in xy_steps]
    ag_order = range(15)
    z_others = [lax.rem(z + i, 8) for i in (4, 3, 5, 2, 6, 1, 7)]
    sides = [(i, j) for i in (-1, 1) for j in (-1, 1, 0)] + [(0, -1), (0, 1)]

    def side_peer(i, j):
        return (lax.rem(g + i + 8, 8), lax.rem(t + j + 32, 32))

    loads = [
        pltpu.make_async_copy(source, target, local_sem.at[i])
        for i, (source, target) in enumerate(
            ((pool_hbm, pool), (tg_hbm, tg), (w1_hbm, w1), (w2_hbm, w2))
        )
    ]
    for load in loads:
        load.start()
    barrier = pltpu.get_barrier_semaphore()

    def greet(who):
        pl.semaphore_signal(barrier, inc=1, device_id=who, device_id_type=MESH)

    for i, j in sides:
        greet(side_peer(i, j))
    for other in xy_others:
        greet(xy_peer(other))
    for other in z_others:
        greet(z_peer(other))
    greet(partner)
    loads[0].wait()
    pad[4:12, 1:9] = pool[...].astype(BF16).reshape(8, 8, 8, C0)
    pl.semaphore_wait(barrier, 31)

    cols_from = {1: (8, 1), 0: (1, 8), -1: (1, 1)}
    cols_to = {1: (0, 1), 0: (1, 8), -1: (9, 1)}

    def halo(i, j, row_from, row_to, rows, arrival):
        (fc, nc), (tc, _) = cols_from[j], cols_to[j]
        return pltpu.make_async_remote_copy(
            src_ref=pad.at[pl.ds(row_from, rows), pl.ds(fc, nc)],
            dst_ref=pad.at[pl.ds(row_to, rows), pl.ds(tc, nc)],
            send_sem=halo_sem.at[0],
            recv_sem=halo_sem.at[arrival],
            device_id=side_peer(i, j),
            device_id_type=MESH,
        )

    near_rows = {1: (10, 2, 2), 0: (4, 4, 8), -1: (4, 12, 2)}
    far_rows = {1: (8, 0, 2), -1: (6, 14, 2)}
    near = [halo(i, j, *near_rows[i], 1) for i, j in sides]
    far = [halo(i, j, *far_rows[i], 2) for i, j in sides if i != 0]
    for copy in near + far:
        copy.start()

    def wait_all(part, sem):
        pltpu.make_async_copy(part, part, sem).wait()

    loads[1].wait()
    for l in range(2):
        whole = tg[l]
        ts[l] = (whole + whole.T) * 0.5
    loads[2].wait()
    loads[3].wait()
    wait_all(pad.at[pl.ds(0, 7), pl.ds(0, 8)], halo_sem.at[1])

    def on_edges(top, bottom, left, right):
        pl.when(g == 0)(top)
        pl.when(g == 7)(bottom)
        pl.when(t == 0)(left)
        pl.when(t == 31)(right)

    def clear_pad(up, down, blocks):
        def zero(first, rows, col, cols):
            pad[first : first + rows, col : col + cols] = jnp.zeros((rows, cols, 8, C0), BF16)

        def column(col):
            for first, rows in blocks:
                zero(first, rows, col, 1)

        on_edges(
            lambda: zero(up, 2, 0, 10),
            lambda: zero(down, 2, 0, 10),
            lambda: column(0),
            lambda: column(9),
        )

    def clear_edges(ref, first, rows, depth):
        def zero(row, n, col, cols):
            ref[row : row + n, col : col + cols] = jnp.zeros((n, cols, ref.shape[2]), ref.dtype)

        on_edges(
            lambda: zero(first, depth, 0, W),
            lambda: zero(first + rows - depth, depth, 0, W),
            lambda: zero(first, rows, 0, 8),
            lambda: zero(first, rows, W - 8, 8),
        )

    clear_pad(2, 12, ((2, 12),))

    def shift_pool(r, carry):
        row = pad[r].astype(F32).reshape(W, C0)
        for b in range(3):
            xs[r, :, b * C0 : (b + 1) * C0] = ahead(row, b - 1).astype(BF16)
        return carry

    def conv1(first, rows):
        total = None
        for a in range(3):
            part = dot_nn(flat(xs[pl.ds(first + a, rows)]), w1[a])
            total = part if total is None else total + part
        pre1[pl.ds(first, rows)] = total.reshape(rows, W, C1)

    def gelu_row(r, carry):
        act1[r] = gelu_value(pre1[r])
        return carry

    lax.fori_loop(2, 14, shift_pool, 0)

    def conv1_step(i, carry):
        conv1(2 + 5 * i, 5)
        return carry

    lax.fori_loop(0, 2, conv1_step, 0)
    lax.fori_loop(2, 12, gelu_row, 0)
    clear_edges(act1, 2, 10, 1)

    def shift_first(r, carry):
        row = act1[r + 2]
        for b in range(3):
            fsm[r, :, b * C1 : (b + 1) * C1] = ahead(row, b - 1)[8:72].astype(BF16)
        return carry

    lax.fori_loop(0, 10, shift_first, 0)

    def remote(source, target, send, recv, who):
        return pltpu.make_async_remote_copy(
            src_ref=source, dst_ref=target, send_sem=send, recv_sem=recv,
            device_id=who, device_id_type=MESH,
        )

    def pair_piece(l):
        return remote(
            s0.at[l, 1 - core], r0.at[l], pair_send.at[l, 0], pair_recv.at[l, 0], partner
        )

    def pair_mean(l):
        own = means.at[l, 2 * k + core]
        return remote(own, own, pair_send.at[l, 1], pair_recv.at[l, 1], partner)

    def pair_mean_in(l):
        other = means.at[l, 2 * k + 1 - core]
        return remote(other, other, pair_send.at[l, 1], pair_recv.at[l, 1], partner)

    def rs_piece(l, other):
        return remote(
            tsum.at[l, other], r1.at[l, k], rs_sem.at[l, 0, 0], rs_sem.at[l, 0, 1], xy_peer(other)
        )

    def rs_mean(l, other):
        both = means.at[l, pl.ds(2 * k, 2)]
        return remote(both, both, rs_sem.at[l, 1, 0], rs_sem.at[l, 1, 1], xy_peer(other))

    def z_piece(l, other):
        part = zb.at[l, z]
        return remote(part, part, z_sem.at[l, 0, 0], z_sem.at[l, 0, 1], z_peer(other))

    def z_mean(l, other):
        part = zm.at[l, z]
        return remote(part, part, z_sem.at[l, 1, 0], z_sem.at[l, 1, 1], z_peer(other))

    def ag_piece(l, n):
        part = ga.at[l, core, k]
        return remote(
            part, part, ag_send.at[l], ag_recv.at[l, n // 4], xy_peer(xy_others[n])
        )

    def fw_piece(l, slot):
        part = ga.at[l, core, slot]
        return remote(part, part, fw_sem.at[l, 0], fw_sem.at[l, 1], partner)

    def local_gram(l, values):
        mean = jnp.sum(values, axis=0, keepdims=True) * (1.0 / OWN)
        means[l, 2 * k + core] = mean
        cen = (values - mean).astype(BF16)
        pair_mean(l).start()
        gram = lax.dot_general(cen, cen, (((0,), (0,)), ((), ())), preferred_element_type=F32)
        for i in range(4):
            for d in range(3):
                j = (i + d) % 4
                block = gram[128 * i : 128 * i + 128, 128 * j : 128 * j + 128].astype(BF16)
                s0[l, i // 2, (i % 2) * 8 : (i % 2) * 8 + 8, :, 128 * d : 128 * d + 128] = (
                    block.reshape(8, 16, 128)
                )
        pair_piece(l).start()

    def rs_start(l):
        pair_mean_in(l).wait_recv()
        for other in xy_others:
            rs_mean(l, other).start()
        pair_piece(l).wait_recv()
        tsum[l] = (s0[l, core].astype(F32) + r0[l].astype(F32)).astype(BF16)
        r1[l, k] = tsum[l, k]
        for other in xy_others:
            rs_piece(l, other).start()

    def spread(rows):
        n = rows.shape[0]
        mean = jnp.sum(rows, axis=0, keepdims=True) * (1.0 / n)
        off = rows - mean
        dxs[0:n, 0:C1] = off
        dxs[0:n, C1:] = off[:, 0:256]
        lane = lax.broadcasted_iota(jnp.int32, (16, C1), 1)
        sub = lax.broadcasted_iota(jnp.int32, (16, C1), 0)
        pick = jnp.where(lane == strip * 16 + sub, 1.0, 0.0).astype(F32)
        left = lax.dot_general(
            pick, off, (((1,), (1,)), ((), ())), precision=HIGHEST, preferred_element_type=F32
        )
        right = dxs[0:n, pl.ds(pl.multiple_of((strip // 8) * 128, 128), 384)]
        return mean, jnp.dot(left, right, precision=HIGHEST, preferred_element_type=F32)

    def plane_done(l):
        wait_all(means.at[l, pl.ds(0, 30)], rs_sem.at[l, 1, 1])
        mean, extra = spread(means[l].reshape(32, C1))
        zm[l, z] = mean
        wait_all(r1.at[l, pl.ds(0, 15)], rs_sem.at[l, 0, 1])
        total = jnp.sum(r1[l].astype(F32), axis=0) + float(OWN) * extra
        zb[l, z] = total.astype(Z_TYPE)
        for other in z_others:
            z_mean(l, other).start()
        for other in z_others:
            z_piece(l, other).start()

    def z_done(l):
        wait_all(zm.at[l, pl.ds(0, 7)], z_sem.at[l, 1, 1])
        mean, extra = spread(zm[l].reshape(8, C1))
        wait_all(zb.at[l, pl.ds(0, 7)], z_sem.at[l, 0, 1])
        total = jnp.sum(zb[l].astype(F32), axis=0) + float(32 * OWN) * extra
        ga[l, core, k] = (total * (1.0 / CELLS)).astype(BF16)
        for n in ag_order:
            ag_piece(l, n).start()
        fw_piece(l, k).start()
        return mean

    def gathered(l):
        for n in ag_order:
            if n % 4 == 0:
                wait_all(ga.at[l, core, pl.ds(0, min(4, 15 - n))], ag_recv.at[l, n // 4])
            fw_piece(l, xy_from[n]).start()

    def forwarded(l):
        wait_all(ga.at[l, 1 - core], fw_sem.at[l, 1])

    def mismatch(l):
        def put(i, j, block):
            block = block - ts[l, 128 * i : 128 * i + 128, 128 * j : 128 * j + 128]
            top = block.astype(BF16)
            sh[l, 128 * i : 128 * i + 128, 128 * j : 128 * j + 128] = top
            sl[l, 128 * i : 128 * i + 128, 128 * j : 128 * j + 128] = (
                block - top.astype(F32)
            ).astype(BF16)

        for i in range(4):
            rows = ga[l, i // 2, (i % 2) * 8 : (i % 2) * 8 + 8].astype(F32).reshape(128, 384)
            for d in range(3):
                block = rows[:, 128 * d : 128 * d + 128]
                put(i, (i + d) % 4, block)
                if d == 1:
                    put((i + 1) % 4, i, block.T)

    local_gram(0, flat(act1[3:11, 8:72, :]))

    def conv2_main(i, carry):
        total = None
        for a in range(3):
            part = dot_nn(flat(fsm[pl.ds(4 * i + a, 4)]), w2[a])
            total = part if total is None else total + part
        act2m[pl.ds(4 * i, 4)] = gelu_value(total).reshape(4, 64, C1)
        return carry

    lax.fori_loop(0, 1, conv2_main, 0)
    rs_start(0)
    lax.fori_loop(1, 2, conv2_main, 0)
    local_gram(1, flat(act2m[...]))

    wait_all(pad.at[pl.ds(0, 5), pl.ds(0, 8)], halo_sem.at[2])
    clear_pad(0, 14, ((0, 2), (14, 2)))
    lax.fori_loop(0, 2, shift_pool, 0)
    lax.fori_loop(14, 16, shift_pool, 0)

    def conv1_rim(i, carry):
        conv1(12 * i, 2)
        return carry

    lax.fori_loop(0, 2, conv1_rim, 0)
    rs_start(1)

    plane_done(0)

    def finish_first(r, carry):
        value, slope = gelu_both(pre1[r])
        act1[r] = value
        sl1[r] = slope
        return carry

    lax.fori_loop(0, 14, finish_first, 0)
    clear_edges(act1, 0, 14, 3)
    clear_edges(sl1, 2, 10, 1)

    def shift_first_all(r, carry):
        row = act1[r]
        for b in range(3):
            fs[r, :, b * C1 : (b + 1) * C1] = ahead(row, b - 1).astype(BF16)
        return carry

    lax.fori_loop(0, 14, shift_first_all, 0)

    plane_done(1)

    def conv2_all(i, carry):
        total = None
        for a in range(3):
            part = dot_nn(flat(fs[pl.ds(4 * i + a, 4)]), w2[a])
            total = part if total is None else total + part
        value, slope = gelu_both(total)
        act2[pl.ds(4 * i, 4)] = value.reshape(4, W, C1)
        sl2[pl.ds(4 * i, 4)] = slope.reshape(4, W, C1)
        return carry

    lax.fori_loop(0, 1, conv2_all, 0)
    mean_first = z_done(0)
    lax.fori_loop(1, 2, conv2_all, 0)
    mean_second = z_done(1)
    lax.fori_loop(2, 3, conv2_all, 0)
    clear_edges(sl2, 0, 12, 2)

    def centre(source, high, low, mean, shift):
        def step(r, carry):
            cen = source[r + shift] - mean
            top = cen.astype(BF16)
            high[r] = top
            low[r] = (cen - top.astype(F32)).astype(BF16)
            return carry

        return step

    lax.fori_loop(0, 10, centre(act1, ch1, cl1, mean_first, 2), 0)
    lax.fori_loop(0, 12, centre(act2, ch2, cl2, mean_second, 0), 0)

    def push(l, high, low, first, rows):
        top = flat(high[pl.ds(first, rows)])
        rest = flat(low[pl.ds(first, rows)])
        return dot_nn(top, sh[l]) + dot_nn(rest, sh[l]) + dot_nn(top, sl[l])

    def push_first(i, carry):
        flow1[pl.ds(5 * i, 5)] = push(0, ch1, cl1, 5 * i, 5).reshape(5, W, C1)
        return carry

    gathered(0)
    wait_all(pad.at[pl.ds(0, 12), pl.ds(0, 8)], halo_sem.at[0])
    for l in range(2):
        pair_piece(l).wait_send()
        pair_mean(l).wait_send()
        wait_all(r1.at[l, pl.ds(0, 15)], rs_sem.at[l, 0, 0])
        wait_all(means.at[l, pl.ds(0, 30)], rs_sem.at[l, 1, 0])
        wait_all(zb.at[l, pl.ds(0, 7)], z_sem.at[l, 0, 0])
        wait_all(zm.at[l, pl.ds(0, 7)], z_sem.at[l, 1, 0])
    forwarded(0)
    mismatch(0)
    lax.fori_loop(0, 1, push_first, 0)
    gathered(1)
    lax.fori_loop(1, 2, push_first, 0)
    forwarded(1)

    mismatch(1)

    def back2(i, carry):
        grad = push(1, ch2, cl2, 4 * i, 4) * flat(sl2[pl.ds(4 * i, 4)])
        for b in range(3):
            gs2[pl.ds(4 * i, 4), :, b * C1 : (b + 1) * C1] = (
                ahead(grad, 1 - b).astype(BF16).reshape(4, W, C1)
            )
        return carry

    lax.fori_loop(0, 3, back2, 0)

    def back1(i, carry):
        flow = flat(flow1[pl.ds(5 * i, 5)])
        for a in range(3):
            for b in range(3):
                flow = flow + dot_nt(
                    flat(gs2[pl.ds(5 * i + 2 - a, 5), :, b * C1 : (b + 1) * C1]),
                    w2[a, b * C1 : (b + 1) * C1, :],
                )
        grad = flow * flat(sl1[pl.ds(5 * i + 2, 5)])
        for b in range(3):
            gs1[pl.ds(5 * i, 5), :, b * C1 : (b + 1) * C1] = (
                ahead(grad, 1 - b).reshape(5, W, C1)[:, 8:72].astype(BF16)
            )
        return carry

    lax.fori_loop(0, 2, back1, 0)

    for l in range(2):
        wait_all(ga.at[l, core, pl.ds(0, 15)], ag_send.at[l])
        wait_all(ga.at[l, core], fw_sem.at[l, 0])

    def back0(i, carry):
        total = None
        for a in range(3):
            for b in range(3):
                part = dot_nt(
                    flat(gs1[pl.ds(4 * i + 2 - a, 4), :, b * C1 : (b + 1) * C1]),
                    w1[a, b * C0 : (b + 1) * C0, :],
                )
                total = part if total is None else total + part
        out[pl.ds(4 * i, 4)] = total.reshape(4, 64, C0)
        return carry

    lax.fori_loop(0, 2, back0, 0)


def local(pool_input, weight_first, weight_second, targets):
    v = pltpu.VMEM
    dma = pltpu.SemaphoreType.DMA
    scratch = [
        v((8, 64, C0), F32),
        v((3, 3 * C0, C1), BF16),
        v((3, 3 * C1, C1), BF16),
        v((2, C1, C1), F32),
        v((2, C1, C1), F32),
        v((16, 10, 8, C0), BF16),
        v((16, W, 3 * C0), BF16),
        v((14, W, C1), F32),
        v((14, W, C1), F32),
        v((14, W, C1), F32),
        v((10, 64, 3 * C1), BF16),
        v((14, W, 3 * C1), BF16),
        v((8, 64, C1), F32),
        v((12, W, C1), F32),
        v((12, W, C1), F32),
        v((10, W, C1), BF16),
        v((10, W, C1), BF16),
        v((12, W, C1), BF16),
        v((12, W, C1), BF16),
        v((2, 2, 16, 16, 384), BF16),
        v((2, 16, 16, 384), BF16),
        v((2, 16, 16, 384), BF16),
        v((2, 16, 16, 384), BF16),
        v((2, 32, 1, C1), F32),
        v((32, C1 + 256), F32),
        v((2, 8, 16, 384), Z_TYPE),
        v((2, 8, 1, C1), F32),
        v((2, 2, 16, 16, 384), BF16),
        v((2, C1, C1), BF16),
        v((2, C1, C1), BF16),
        dma((4,)),
        dma((3,)),
        dma((2, 2)),
        dma((2, 2)),
        dma((2, 2, 2)),
        dma((2, 2, 2)),
        dma((2,)),
        dma((2, 4)),
        dma((2, 2)),
    ]
    return pl.pallas_call(
        kernel,
        out_shape=pltpu.VMEM((8, 64, C0), F32),
        in_specs=[pl.BlockSpec(memory_space=pltpu.HBM)] * 4,
        out_specs=pl.BlockSpec(memory_space=pltpu.VMEM),
        scratch_shapes=scratch,
        compiler_params=pltpu.CompilerParams(
            collective_id=0, has_side_effects=True, vmem_limit_bytes=67043328 - 768 * 1024
        ),
        name="style_grad",
    )(
        pool_input,
        weight_first.reshape(3, 3 * C0, C1),
        weight_second.reshape(3, 3 * C1, C1),
        targets,
    )


def solution(mesh):
    return jax.shard_map(
        local,
        mesh=mesh,
        in_specs=(P("grp", "tile", None), P(), P(), P()),
        out_specs=P("grp", "tile", None),
        check_vma=False,
    )
```

```python
import functools

import jax
import jax.numpy as jnp
from jax import lax
from jax.experimental import pallas as pl
from jax.experimental.pallas import tpu as pltpu
from jax.sharding import PartitionSpec as P

GELU_SCALE = 0.7978845608
GELU_CUBIC = 0.044715
F32 = jnp.float32
BF16 = jnp.bfloat16
HIGHEST = lax.Precision.HIGHEST
MESH = pl.DeviceIdType.MESH
Z_TYPE = BF16
CELLS = 64 * 2048
OWN = 512
C0, C1 = 256, 512
W = 80


def gelu_value(z):
    return 0.5 * z * (1.0 + jnp.tanh(GELU_SCALE * (z + GELU_CUBIC * (z * z * z))))


def gelu_both(z):
    square = z * z
    hyper = jnp.tanh(GELU_SCALE * (z + GELU_CUBIC * (square * z)))
    half = 0.5 * (1.0 + hyper)
    slope = half + 0.5 * z * (1.0 - hyper * hyper) * GELU_SCALE * (1.0 + 3.0 * GELU_CUBIC * square)
    return z * half, slope


def flat(block):
    return block.reshape(block.shape[0] * block.shape[1], block.shape[2])


def dot_nn(left, right):
    return jnp.dot(left, right, preferred_element_type=F32)


def dot_nt(left, right):
    return lax.dot_general(left, right, (((1,), (1,)), ((), ())), preferred_element_type=F32)


def ahead(x, step):
    return x if step == 0 else pltpu.roll(x, (-step) % x.shape[0], 0)


def kernel(
    pool_hbm, w1_hbm, w2_hbm, tg_hbm, out,
    pool, w1, w2, tg, ts, pad, xs, pre1, act1, sl1, fsm, fs, act2m, act2, sl2,
    ch1, cl1, ch2, cl2, s0, r0, tsum, r1, means, dxs, zb, zm, ga, sh, sl,
    local_sem, halo_sem, pair_send, pair_recv, rs_sem, z_sem, ag_send, ag_recv, fw_sem,
):
    gs1, gs2, flow1 = fsm, fs, pre1
    g = lax.axis_index("grp")
    t = lax.axis_index("tile")
    core = lax.rem(t, 2)
    x = lax.rem(t // 2, 2) * 2 + g // 4
    y = lax.rem(g, 4)
    z = t // 4
    k = x * 4 + y
    strip = core * 16 + k

    def device(x_to, y_to, z_to, core_to):
        return (lax.rem(x_to, 2) * 4 + y_to, z_to * 4 + (x_to // 2) * 2 + core_to)

    partner = device(x, y, z, 1 - core)

    def xy_peer(other):
        return device(other // 4, lax.rem(other, 4), z, core)

    def z_peer(other):
        return device(x, y, other, core)

    xy_steps = sorted(
        ((i, j) for i in range(4) for j in range(4) if (i, j) != (0, 0)),
        key=lambda s: -(min(s[0], 4 - s[0]) + min(s[1], 4 - s[1])),
    )
    xy_others = [lax.rem(x + i, 4) * 4 + lax.rem(y + j, 4) for i, j in xy_steps]
    xy_from = [lax.rem(x + 4 - i, 4) * 4 + lax.rem(y + 4 - j, 4) for i, j in xy_steps]
    z_others = [lax.rem(z + i, 8) for i in (4, 3, 5, 2, 6, 1, 7)]
    sides = [(i, j) for i in (-1, 1) for j in (-1, 1, 0)] + [(0, -1), (0, 1)]

    def side_peer(i, j):
        return (lax.rem(g + i + 8, 8), lax.rem(t + j + 32, 32))

    loads = [
        pltpu.make_async_copy(source, target, local_sem.at[i])
        for i, (source, target) in enumerate(
            ((pool_hbm, pool), (w1_hbm, w1), (tg_hbm, tg), (w2_hbm, w2))
        )
    ]
    for load in loads:
        load.start()
    barrier = pltpu.get_barrier_semaphore()

    def greet(who):
        pl.semaphore_signal(barrier, inc=1, device_id=who, device_id_type=MESH)

    for i, j in sides:
        greet(side_peer(i, j))
    for other in xy_others:
        greet(xy_peer(other))
    for other in z_others:
        greet(z_peer(other))
    greet(partner)
    loads[0].wait()
    pad[4:12, 1:9] = pool[...].astype(BF16).reshape(8, 8, 8, C0)
    pl.semaphore_wait(barrier, 31)

    cols_from = {1: (8, 1), 0: (1, 8), -1: (1, 1)}
    cols_to = {1: (0, 1), 0: (1, 8), -1: (9, 1)}

    def halo(i, j, row_from, row_to, rows, arrival):
        (fc, nc), (tc, _) = cols_from[j], cols_to[j]
        return pltpu.make_async_remote_copy(
            src_ref=pad.at[pl.ds(row_from, rows), pl.ds(fc, nc)],
            dst_ref=pad.at[pl.ds(row_to, rows), pl.ds(tc, nc)],
            send_sem=halo_sem.at[0],
            recv_sem=halo_sem.at[arrival],
            device_id=side_peer(i, j),
            device_id_type=MESH,
        )

    near_rows = {1: (10, 2, 2), 0: (4, 4, 8), -1: (4, 12, 2)}
    far_rows = {1: (8, 0, 2), -1: (6, 14, 2)}
    near = [halo(i, j, *near_rows[i], 1) for i, j in sides]
    far = [halo(i, j, *far_rows[i], 2) for i, j in sides if i != 0]
    for copy in near + far:
        copy.start()

    def wait_all(part, sem):
        pltpu.make_async_copy(part, part, sem).wait()

    def conv1_from(pieces):
        total = None
        for a in range(3):
            left = [flat(xs[pl.ds(row + a, rows), col : col + cols]) for row, rows, col, cols in pieces]
            part = dot_nn(jnp.concatenate(left, axis=0) if len(left) > 1 else left[0], w1[a])
            total = part if total is None else total + part
        at = 0
        for row, rows, col, cols in pieces:
            n = rows * cols
            pre1[pl.ds(row, rows), col : col + cols] = total[at : at + n].reshape(rows, cols, C1)
            at += n

    def shift_inner(r, carry):
        row = pool[r - 4].astype(BF16).astype(F32)
        for b in range(3):
            xs[r, 16:64, b * C0 : (b + 1) * C0] = ahead(row, b - 1)[8:56].astype(BF16)
        return carry

    def gelu_inner(r, carry):
        act1[r, 16:64] = gelu_value(pre1[r, 16:64])
        return carry

    lax.fori_loop(4, 12, shift_inner, 0)
    loads[1].wait()
    conv1_from([(4, 6, 16, 48)])
    lax.fori_loop(4, 10, gelu_inner, 0)
    loads[2].wait()
    for l in range(2):
        whole = tg[l]
        ts[l] = (whole + whole.T) * 0.5
    wait_all(pad.at[pl.ds(0, 7), pl.ds(0, 8)], halo_sem.at[1])

    def on_edges(top, bottom, left, right):
        pl.when(g == 0)(top)
        pl.when(g == 7)(bottom)
        pl.when(t == 0)(left)
        pl.when(t == 31)(right)

    def clear_pad(up, down, blocks):
        def zero(first, rows, col, cols):
            pad[first : first + rows, col : col + cols] = jnp.zeros((rows, cols, 8, C0), BF16)

        def column(col):
            for first, rows in blocks:
                zero(first, rows, col, 1)

        on_edges(
            lambda: zero(up, 2, 0, 10),
            lambda: zero(down, 2, 0, 10),
            lambda: column(0),
            lambda: column(9),
        )

    def clear_edges(ref, first, rows, depth):
        def zero(row, n, col, cols):
            ref[row : row + n, col : col + cols] = jnp.zeros((n, cols, ref.shape[2]), ref.dtype)

        on_edges(
            lambda: zero(first, depth, 0, W),
            lambda: zero(first + rows - depth, depth, 0, W),
            lambda: zero(first, rows, 0, 8),
            lambda: zero(first, rows, W - 8, 8),
        )

    clear_pad(2, 12, ((2, 12),))

    def shift_pool(r, carry):
        row = pad[r].astype(F32).reshape(W, C0)
        for b in range(3):
            xs[r, :, b * C0 : (b + 1) * C0] = ahead(row, b - 1).astype(BF16)
        return carry

    def gelu_row(r, carry):
        act1[r] = gelu_value(pre1[r])
        return carry

    def gelu_sides(r, carry):
        for col in (0, 64):
            act1[r, col : col + 16] = gelu_value(pre1[r, col : col + 16])
        return carry

    lax.fori_loop(2, 14, shift_pool, 0)
    conv1_from([(2, 2, 0, W), (10, 2, 0, W), (4, 6, 0, 16), (4, 6, 64, 16)])
    lax.fori_loop(2, 4, gelu_row, 0)
    lax.fori_loop(4, 10, gelu_sides, 0)
    lax.fori_loop(10, 12, gelu_row, 0)
    clear_edges(act1, 2, 10, 1)

    def shift_first(r, carry):
        row = act1[r + 2]
        for b in range(3):
            fsm[r, :, b * C1 : (b + 1) * C1] = ahead(row, b - 1)[8:72].astype(BF16)
        return carry

    lax.fori_loop(0, 10, shift_first, 0)

    def remote(source, target, send, recv, who):
        return pltpu.make_async_remote_copy(
            src_ref=source, dst_ref=target, send_sem=send, recv_sem=recv,
            device_id=who, device_id_type=MESH,
        )

    def by_core(who, act):
        pl.when(who == 0)(lambda: act(pl.ds(0, 384)))
        pl.when(who == 1)(lambda: act(pl.ds(0, 256)))

    def pair_piece(l, lanes):
        return remote(
            s0.at[l, 1 - core, :, :, lanes],
            r0.at[l, :, :, lanes],
            pair_send.at[l, 0],
            pair_recv.at[l, 0],
            partner,
        )

    def pair_mean(l):
        own = means.at[l, 2 * k + core]
        return remote(own, own, pair_send.at[l, 1], pair_recv.at[l, 1], partner)

    def pair_mean_in(l):
        other = means.at[l, 2 * k + 1 - core]
        return remote(other, other, pair_send.at[l, 1], pair_recv.at[l, 1], partner)

    def rs_piece(l, other, lanes):
        return remote(
            tsum.at[l, other, :, lanes], r1.at[l, k, :, lanes], rs_sem.at[l, 0, 0], rs_sem.at[l, 0, 1], xy_peer(other)
        )

    def rs_mean(l, other):
        both = means.at[l, pl.ds(2 * k, 2)]
        return remote(both, both, rs_sem.at[l, 1, 0], rs_sem.at[l, 1, 1], xy_peer(other))

    def z_piece(l, other, lanes):
        part = zb.at[l, z, :, lanes]
        return remote(part, part, z_sem.at[l, 0, 0], z_sem.at[l, 0, 1], z_peer(other))

    def z_mean(l, other):
        part = zm.at[l, z]
        return remote(part, part, z_sem.at[l, 1, 0], z_sem.at[l, 1, 1], z_peer(other))

    def ag_piece(l, n, lanes):
        part = ga.at[l, core, k, :, lanes]
        return remote(
            part, part, ag_send.at[l], ag_recv.at[l, n // 4], xy_peer(xy_others[n])
        )

    def fw_piece(l, slot, lanes):
        part = ga.at[l, core, slot, :, lanes]
        return remote(part, part, fw_sem.at[l, 0], fw_sem.at[l, 1], partner)

    def local_gram(l, values):
        mean = jnp.sum(values, axis=0, keepdims=True) * (1.0 / OWN)
        means[l, 2 * k + core] = mean
        cen = (values - mean).astype(BF16)
        pair_mean(l).start()
        gram = lax.dot_general(cen, cen, (((0,), (0,)), ((), ())), preferred_element_type=F32)
        for i in range(4):
            for d in range(3 if i < 2 else 2):
                j = (i + d) % 4
                block = gram[128 * i : 128 * i + 128, 128 * j : 128 * j + 128].astype(BF16)
                s0[l, i // 2, (i % 2) * 8 : (i % 2) * 8 + 8, :, 128 * d : 128 * d + 128] = (
                    block.reshape(8, 16, 128)
                )
        by_core(1 - core, lambda lanes: pair_piece(l, lanes).start())

    def rs_start(l):
        pair_mean_in(l).wait_recv()
        for other in xy_others:
            rs_mean(l, other).start()
        by_core(core, lambda lanes: wait_all(r0.at[l, :, :, lanes], pair_recv.at[l, 0]))
        tsum[l] = (s0[l, core].astype(F32) + r0[l].astype(F32)).astype(BF16)
        r1[l, k] = tsum[l, k]

        def send(lanes):
            for other in xy_others:
                rs_piece(l, other, lanes).start()

        by_core(core, send)

    def spread(rows):
        n = rows.shape[0]
        mean = jnp.sum(rows, axis=0, keepdims=True) * (1.0 / n)
        off = rows - mean
        dxs[0:n, 0:C1] = off
        dxs[0:n, C1:] = off[:, 0:256]
        lane = lax.broadcasted_iota(jnp.int32, (16, C1), 1)
        sub = lax.broadcasted_iota(jnp.int32, (16, C1), 0)
        pick = jnp.where(lane == strip * 16 + sub, 1.0, 0.0).astype(F32)
        left = lax.dot_general(
            pick, off, (((1,), (1,)), ((), ())), precision=HIGHEST, preferred_element_type=F32
        )
        right = dxs[0:n, pl.ds(pl.multiple_of((strip // 8) * 128, 128), 384)]
        return mean, jnp.dot(left, right, precision=HIGHEST, preferred_element_type=F32)

    def plane_done(l):
        wait_all(means.at[l, pl.ds(0, 30)], rs_sem.at[l, 1, 1])
        mean, extra = spread(means[l].reshape(32, C1))
        zm[l, z] = mean
        by_core(
            core,
            lambda lanes: wait_all(r1.at[l, pl.ds(0, 15), :, lanes], rs_sem.at[l, 0, 1]),
        )
        for other in z_others:
            z_mean(l, other).start()
        total = jnp.sum(r1[l].astype(F32), axis=0) + float(OWN) * extra
        zb[l, z] = total.astype(Z_TYPE)

        def send(lanes):
            for other in z_others:
                z_piece(l, other, lanes).start()

        by_core(core, send)

    def z_done(l):
        wait_all(zm.at[l, pl.ds(0, 7)], z_sem.at[l, 1, 1])
        mean, extra = spread(zm[l].reshape(8, C1))
        by_core(
            core, lambda lanes: wait_all(zb.at[l, pl.ds(0, 7), :, lanes], z_sem.at[l, 0, 1])
        )
        total = jnp.sum(zb[l].astype(F32), axis=0) + float(32 * OWN) * extra
        ga[l, core, k] = (total * (1.0 / CELLS)).astype(BF16)

        def send(lanes):
            for n in range(15):
                ag_piece(l, n, lanes).start()
            fw_piece(l, k, lanes).start()

        by_core(core, send)
        return mean

    def gathered(l):
        def forward(lanes):
            for n in range(15):
                if n % 4 == 0:
                    wait_all(
                        ga.at[l, core, pl.ds(0, min(4, 15 - n)), :, lanes], ag_recv.at[l, n // 4]
                    )
                fw_piece(l, xy_from[n], lanes).start()

        by_core(core, forward)

    def forwarded(l):
        by_core(1 - core, lambda lanes: wait_all(ga.at[l, 1 - core, :, :, lanes], fw_sem.at[l, 1]))

    def mismatch(l):
        def put(i, j, block):
            block = block - ts[l, 128 * i : 128 * i + 128, 128 * j : 128 * j + 128]
            top = block.astype(BF16)
            sh[l, 128 * i : 128 * i + 128, 128 * j : 128 * j + 128] = top
            sl[l, 128 * i : 128 * i + 128, 128 * j : 128 * j + 128] = (
                block - top.astype(F32)
            ).astype(BF16)

        for i in range(4):
            for d in range(3 if i < 2 else 2):
                block = ga[l, i // 2, (i % 2) * 8 : (i % 2) * 8 + 8, :, 128 * d : 128 * d + 128]
                block = block.astype(F32).reshape(128, 128)
                put(i, (i + d) % 4, block)
                if d > 0:
                    put((i + d) % 4, i, block.T)

    local_gram(0, flat(act1[3:11, 8:72, :]))

    loads[3].wait()

    def conv2_main(i, carry):
        total = None
        for a in range(3):
            part = dot_nn(flat(fsm[pl.ds(4 * i + a, 4)]), w2[a])
            total = part if total is None else total + part
        act2m[pl.ds(4 * i, 4)] = gelu_value(total).reshape(4, 64, C1)
        return carry

    lax.fori_loop(0, 1, conv2_main, 0)
    rs_start(0)
    lax.fori_loop(1, 2, conv2_main, 0)
    local_gram(1, flat(act2m[...]))

    wait_all(pad.at[pl.ds(0, 5), pl.ds(0, 8)], halo_sem.at[2])
    clear_pad(0, 14, ((0, 2), (14, 2)))
    lax.fori_loop(0, 2, shift_pool, 0)
    lax.fori_loop(14, 16, shift_pool, 0)

    conv1_from([(0, 2, 0, W), (12, 2, 0, W)])
    rs_start(1)

    def finish_first(r, carry):
        value, slope = gelu_both(pre1[r])
        act1[r] = value
        sl1[r] = slope
        return carry

    def shift_first_all(r, carry):
        row = act1[r]
        for b in range(3):
            fs[r, :, b * C1 : (b + 1) * C1] = ahead(row, b - 1).astype(BF16)
        return carry

    def conv2_all(i, carry):
        total = None
        for a in range(3):
            part = dot_nn(flat(fs[pl.ds(3 * i + a, 3)]), w2[a])
            total = part if total is None else total + part
        value, slope = gelu_both(total)
        act2[pl.ds(3 * i, 3)] = value.reshape(3, W, C1)
        sl2[pl.ds(3 * i, 3)] = slope.reshape(3, W, C1)
        return carry

    lax.fori_loop(0, 14, finish_first, 0)
    clear_edges(act1, 0, 14, 3)
    clear_edges(sl1, 2, 10, 1)
    plane_done(0)
    lax.fori_loop(0, 14, shift_first_all, 0)
    lax.fori_loop(0, 1, conv2_all, 0)
    plane_done(1)
    lax.fori_loop(1, 2, conv2_all, 0)
    mean_first = z_done(0)
    lax.fori_loop(2, 3, conv2_all, 0)
    mean_second = z_done(1)
    lax.fori_loop(3, 4, conv2_all, 0)
    clear_edges(sl2, 0, 12, 2)

    def centre(source, high, low, mean, shift):
        def step(r, carry):
            cen = source[r + shift] - mean
            top = cen.astype(BF16)
            high[r] = top
            low[r] = (cen - top.astype(F32)).astype(BF16)
            return carry

        return step

    lax.fori_loop(0, 10, centre(act1, ch1, cl1, mean_first, 2), 0)
    lax.fori_loop(0, 12, centre(act2, ch2, cl2, mean_second, 0), 0)

    def push(l, high, low, first, rows):
        top = flat(high[pl.ds(first, rows)])
        rest = flat(low[pl.ds(first, rows)])
        return dot_nn(top, sh[l]) + dot_nn(rest, sh[l]) + dot_nn(top, sl[l])

    def push_first(i, carry):
        flow1[pl.ds(5 * i, 5)] = push(0, ch1, cl1, 5 * i, 5).reshape(5, W, C1)
        return carry

    gathered(0)
    wait_all(pad.at[pl.ds(0, 12), pl.ds(0, 8)], halo_sem.at[0])
    for l in range(2):
        by_core(1 - core, lambda lanes: wait_all(r0.at[l, :, :, lanes], pair_send.at[l, 0]))
        pair_mean(l).wait_send()

        def sent(lanes):
            wait_all(r1.at[l, pl.ds(0, 15), :, lanes], rs_sem.at[l, 0, 0])
            wait_all(zb.at[l, pl.ds(0, 7), :, lanes], z_sem.at[l, 0, 0])

        by_core(core, sent)
        wait_all(means.at[l, pl.ds(0, 30)], rs_sem.at[l, 1, 0])
        wait_all(zm.at[l, pl.ds(0, 7)], z_sem.at[l, 1, 0])
    forwarded(0)
    mismatch(0)
    lax.fori_loop(0, 1, push_first, 0)
    gathered(1)
    lax.fori_loop(1, 2, push_first, 0)
    forwarded(1)

    mismatch(1)

    def back2(i, carry):
        grad = push(1, ch2, cl2, 4 * i, 4) * flat(sl2[pl.ds(4 * i, 4)])
        for b in range(3):
            gs2[pl.ds(4 * i, 4), :, b * C1 : (b + 1) * C1] = (
                ahead(grad, 1 - b).astype(BF16).reshape(4, W, C1)
            )
        return carry

    lax.fori_loop(0, 3, back2, 0)

    def back1(i, carry):
        flow = flat(flow1[pl.ds(5 * i, 5)])
        for a in range(3):
            for b in range(3):
                flow = flow + dot_nt(
                    flat(gs2[pl.ds(5 * i + 2 - a, 5), :, b * C1 : (b + 1) * C1]),
                    w2[a, b * C1 : (b + 1) * C1, :],
                )
        grad = flow * flat(sl1[pl.ds(5 * i + 2, 5)])
        for b in range(3):
            gs1[pl.ds(5 * i, 5), :, b * C1 : (b + 1) * C1] = (
                ahead(grad, 1 - b).reshape(5, W, C1)[:, 8:72].astype(BF16)
            )
        return carry

    lax.fori_loop(0, 2, back1, 0)

    for l in range(2):

        def gone(lanes):
            wait_all(ga.at[l, core, pl.ds(0, 15), :, lanes], ag_send.at[l])
            wait_all(ga.at[l, core, :, :, lanes], fw_sem.at[l, 0])

        by_core(core, gone)

    def back0(i, carry):
        total = None
        for a in range(3):
            for b in range(3):
                part = dot_nt(
                    flat(gs1[pl.ds(4 * i + 2 - a, 4), :, b * C1 : (b + 1) * C1]),
                    w1[a, b * C0 : (b + 1) * C0, :],
                )
                total = part if total is None else total + part
        out[pl.ds(4 * i, 4)] = total.reshape(4, 64, C0)
        return carry

    lax.fori_loop(0, 2, back0, 0)


def local(pool_input, weight_first, weight_second, targets):
    v = pltpu.VMEM
    dma = pltpu.SemaphoreType.DMA
    scratch = [
        v((8, 64, C0), F32),
        v((3, 3 * C0, C1), BF16),
        v((3, 3 * C1, C1), BF16),
        v((2, C1, C1), F32),
        v((2, C1, C1), F32),
        v((16, 10, 8, C0), BF16),
        v((16, W, 3 * C0), BF16),
        v((14, W, C1), F32),
        v((14, W, C1), F32),
        v((14, W, C1), F32),
        v((10, 64, 3 * C1), BF16),
        v((14, W, 3 * C1), BF16),
        v((8, 64, C1), F32),
        v((12, W, C1), F32),
        v((12, W, C1), F32),
        v((10, W, C1), BF16),
        v((10, W, C1), BF16),
        v((12, W, C1), BF16),
        v((12, W, C1), BF16),
        v((2, 2, 16, 16, 384), BF16),
        v((2, 16, 16, 384), BF16),
        v((2, 16, 16, 384), BF16),
        v((2, 16, 16, 384), BF16),
        v((2, 32, 1, C1), F32),
        v((32, C1 + 256), F32),
        v((2, 8, 16, 384), Z_TYPE),
        v((2, 8, 1, C1), F32),
        v((2, 2, 16, 16, 384), BF16),
        v((2, C1, C1), BF16),
        v((2, C1, C1), BF16),
        dma((4,)),
        dma((3,)),
        dma((2, 2)),
        dma((2, 2)),
        dma((2, 2, 2)),
        dma((2, 2, 2)),
        dma((2,)),
        dma((2, 4)),
        dma((2, 2)),
    ]
    return pl.pallas_call(
        kernel,
        out_shape=pltpu.VMEM((8, 64, C0), F32),
        in_specs=[pl.BlockSpec(memory_space=pltpu.HBM)] * 4,
        out_specs=pl.BlockSpec(memory_space=pltpu.VMEM),
        scratch_shapes=scratch,
        compiler_params=pltpu.CompilerParams(
            collective_id=0, has_side_effects=True, vmem_limit_bytes=67043328 - 768 * 1024
        ),
        name="style_grad",
    )(
        pool_input,
        weight_first.reshape(3, 3 * C0, C1),
        weight_second.reshape(3, 3 * C1, C1),
        targets,
    )


def solution(mesh):
    return jax.shard_map(
        local,
        mesh=mesh,
        in_specs=(P("grp", "tile", None), P(), P(), P()),
        out_specs=P("grp", "tile", None),
        check_vma=False,
    )
```

```python
import functools

import jax
import jax.numpy as jnp
from jax import lax
from jax.experimental import pallas as pl
from jax.experimental.pallas import tpu as pltpu
from jax.sharding import PartitionSpec as P

GELU_SCALE = 0.7978845608
GELU_CUBIC = 0.044715
F32 = jnp.float32
BF16 = jnp.bfloat16
HIGHEST = lax.Precision.HIGHEST
MESH = pl.DeviceIdType.MESH
Z_TYPE = BF16
CELLS = 64 * 2048
OWN = 512
C0, C1 = 256, 512
W = 80


def gelu_value(z):
    return 0.5 * z * (1.0 + jnp.tanh(GELU_SCALE * (z + GELU_CUBIC * (z * z * z))))


def gelu_both(z):
    square = z * z
    hyper = jnp.tanh(GELU_SCALE * (z + GELU_CUBIC * (square * z)))
    half = 0.5 * (1.0 + hyper)
    slope = half + 0.5 * z * (1.0 - hyper * hyper) * GELU_SCALE * (1.0 + 3.0 * GELU_CUBIC * square)
    return z * half, slope


def flat(block):
    return block.reshape(block.shape[0] * block.shape[1], block.shape[2])


def dot_nn(left, right):
    return jnp.dot(left, right, preferred_element_type=F32)


def dot_nt(left, right):
    return lax.dot_general(left, right, (((1,), (1,)), ((), ())), preferred_element_type=F32)


def ahead(x, step):
    return x if step == 0 else pltpu.roll(x, (-step) % x.shape[0], 0)


def kernel(
    pool_hbm, w1_hbm, w2_hbm, tg_hbm, out,
    pool, w1, w2, tg, ts, pad, xs, pre1, act1, sl1, fsm, fs, act2m, act2, sl2,
    ch1, cl1, ch2, cl2, s0, r0, tsum, r1, means, dxs, zb, zm, ga, sh, sl,
    local_sem, halo_sem, pair_send, pair_recv, rs_sem, z_sem, ag_send, ag_recv, fw_sem,
):
    gs1, gs2, flow1 = fsm, fs, pre1
    g = lax.axis_index("grp")
    t = lax.axis_index("tile")
    core = lax.rem(t, 2)
    x = lax.rem(t // 2, 2) * 2 + g // 4
    y = lax.rem(g, 4)
    z = t // 4
    k = x * 4 + y
    strip = core * 16 + k

    def device(x_to, y_to, z_to, core_to):
        return (lax.rem(x_to, 2) * 4 + y_to, z_to * 4 + (x_to // 2) * 2 + core_to)

    partner = device(x, y, z, 1 - core)

    def xy_peer(other):
        return device(other // 4, lax.rem(other, 4), z, core)

    def z_peer(other):
        return device(x, y, other, core)

    xy_steps = sorted(
        ((i, j) for i in range(4) for j in range(4) if (i, j) != (0, 0)),
        key=lambda s: -(min(s[0], 4 - s[0]) + min(s[1], 4 - s[1])),
    )
    xy_others = [lax.rem(x + i, 4) * 4 + lax.rem(y + j, 4) for i, j in xy_steps]
    xy_from = [lax.rem(x + 4 - i, 4) * 4 + lax.rem(y + 4 - j, 4) for i, j in xy_steps]
    z_others = [lax.rem(z + i, 8) for i in (4, 3, 5, 2, 6, 1, 7)]
    sides = [(i, j) for i in (-1, 1) for j in (-1, 1, 0)] + [(0, -1), (0, 1)]

    def side_peer(i, j):
        return (lax.rem(g + i + 8, 8), lax.rem(t + j + 32, 32))

    loads = [
        pltpu.make_async_copy(source, target, local_sem.at[i])
        for i, (source, target) in enumerate(
            ((pool_hbm, pool), (w1_hbm, w1), (tg_hbm, tg), (w2_hbm, w2))
        )
    ]
    for load in loads[:2]:
        load.start()
    barrier = pltpu.get_barrier_semaphore()

    def greet(who):
        pl.semaphore_signal(barrier, inc=1, device_id=who, device_id_type=MESH)

    for i, j in sides:
        greet(side_peer(i, j))
    for other in xy_others:
        greet(xy_peer(other))
    for other in z_others:
        greet(z_peer(other))
    greet(partner)
    loads[0].wait()
    pad[4:12, 1:9] = pool[...].astype(BF16).reshape(8, 8, 8, C0)
    def rows_loop(first, last, step, at_once):
        def some(i, carry):
            for n in range(at_once):
                step(first + i * at_once + n, carry)
            return carry

        times = (last - first) // at_once
        lax.fori_loop(0, times, some, 0, unroll=times == 1)

    def conv1_from(pieces):
        total = None
        for a in range(3):
            left = [flat(xs[pl.ds(row + a, rows), col : col + cols]) for row, rows, col, cols in pieces]
            part = dot_nn(jnp.concatenate(left, axis=0) if len(left) > 1 else left[0], w1[a])
            total = part if total is None else total + part
        at = 0
        for row, rows, col, cols in pieces:
            n = rows * cols
            pre1[pl.ds(row, rows), col : col + cols] = total[at : at + n].reshape(rows, cols, C1)
            at += n

    def shift_inner(r, carry):
        row = pool[r - 4].astype(BF16).astype(F32)
        for b in range(3):
            xs[r, 16:64, b * C0 : (b + 1) * C0] = ahead(row, b - 1)[8:56].astype(BF16)
        return carry

    def gelu_inner(r, carry):
        act1[r, 16:64] = gelu_value(pre1[r, 16:64])
        return carry

    rows_loop(4, 12, shift_inner, 4)
    loads[1].wait()
    for load in loads[2:]:
        load.start()
    conv1_from([(4, 6, 16, 48)])
    rows_loop(4, 10, gelu_inner, 3)
    pl.semaphore_wait(barrier, 31)

    cols_from = {1: (8, 1), 0: (1, 8), -1: (1, 1)}
    cols_to = {1: (0, 1), 0: (1, 8), -1: (9, 1)}

    def halo(i, j, row_from, row_to, rows, arrival):
        (fc, nc), (tc, _) = cols_from[j], cols_to[j]
        return pltpu.make_async_remote_copy(
            src_ref=pad.at[pl.ds(row_from, rows), pl.ds(fc, nc)],
            dst_ref=pad.at[pl.ds(row_to, rows), pl.ds(tc, nc)],
            send_sem=halo_sem.at[0],
            recv_sem=halo_sem.at[arrival],
            device_id=side_peer(i, j),
            device_id_type=MESH,
        )

    near_rows = {1: (10, 2, 2), 0: (4, 4, 8), -1: (4, 12, 2)}
    far_rows = {1: (8, 0, 2), -1: (6, 14, 2)}
    near = [halo(i, j, *near_rows[i], 1) for i, j in sides]
    far = [halo(i, j, *far_rows[i], 2) for i, j in sides if i != 0]
    for copy in near + far:
        copy.start()

    def wait_all(part, sem):
        pltpu.make_async_copy(part, part, sem).wait()

    loads[2].wait()
    for l in range(2):
        whole = tg[l]
        ts[l] = (whole + whole.T) * 0.5
    wait_all(pad.at[pl.ds(0, 7), pl.ds(0, 8)], halo_sem.at[1])

    def on_edges(top, bottom, left, right):
        pl.when(g == 0)(top)
        pl.when(g == 7)(bottom)
        pl.when(t == 0)(left)
        pl.when(t == 31)(right)

    def clear_pad(up, down, blocks):
        def zero(first, rows, col, cols):
            pad[first : first + rows, col : col + cols] = jnp.zeros((rows, cols, 8, C0), BF16)

        def column(col):
            for first, rows in blocks:
                zero(first, rows, col, 1)

        on_edges(
            lambda: zero(up, 2, 0, 10),
            lambda: zero(down, 2, 0, 10),
            lambda: column(0),
            lambda: column(9),
        )

    def clear_edges(ref, first, rows, depth):
        def zero(row, n, col, cols):
            ref[row : row + n, col : col + cols] = jnp.zeros((n, cols, ref.shape[2]), ref.dtype)

        on_edges(
            lambda: zero(first, depth, 0, W),
            lambda: zero(first + rows - depth, depth, 0, W),
            lambda: zero(first, rows, 0, 8),
            lambda: zero(first, rows, W - 8, 8),
        )

    clear_pad(2, 12, ((2, 12),))

    def shift_pool(r, carry):
        row = pad[r].astype(F32).reshape(W, C0)
        for b in range(3):
            xs[r, :, b * C0 : (b + 1) * C0] = ahead(row, b - 1).astype(BF16)
        return carry

    def gelu_row(r, carry):
        act1[r] = gelu_value(pre1[r])
        return carry

    def gelu_sides(r, carry):
        for col in (0, 64):
            act1[r, col : col + 16] = gelu_value(pre1[r, col : col + 16])
        return carry

    rows_loop(2, 14, shift_pool, 4)
    conv1_from([(2, 2, 0, W), (10, 2, 0, W)])
    rows_loop(2, 4, gelu_row, 2)
    rows_loop(10, 12, gelu_row, 2)
    conv1_from([(4, 6, 0, 16), (4, 6, 64, 16)])
    rows_loop(4, 10, gelu_sides, 6)
    clear_edges(act1, 2, 10, 1)

    def shift_first(r, carry):
        row = act1[r + 2]
        for b in range(3):
            fsm[r, :, b * C1 : (b + 1) * C1] = ahead(row, b - 1)[8:72].astype(BF16)
        return carry

    rows_loop(0, 10, shift_first, 5)

    def remote(source, target, send, recv, who):
        return pltpu.make_async_remote_copy(
            src_ref=source, dst_ref=target, send_sem=send, recv_sem=recv,
            device_id=who, device_id_type=MESH,
        )

    def by_core(who, act):
        pl.when(who == 0)(lambda: act(pl.ds(0, 384)))
        pl.when(who == 1)(lambda: act(pl.ds(0, 256)))

    def pair_piece(l, lanes):
        return remote(
            s0.at[l, 1 - core, :, :, lanes],
            r0.at[l, :, :, lanes],
            pair_send.at[l, 0],
            pair_recv.at[l, 0],
            partner,
        )

    def pair_mean(l):
        own = means.at[l, 2 * k + core]
        return remote(own, own, pair_send.at[l, 1], pair_recv.at[l, 1], partner)

    def pair_mean_in(l):
        other = means.at[l, 2 * k + 1 - core]
        return remote(other, other, pair_send.at[l, 1], pair_recv.at[l, 1], partner)

    def rs_piece(l, other, lanes):
        return remote(
            tsum.at[l, other, :, lanes], r1.at[l, k, :, lanes], rs_sem.at[l, 0, 0], rs_sem.at[l, 0, 1], xy_peer(other)
        )

    def rs_mean(l, other):
        both = means.at[l, pl.ds(2 * k, 2)]
        return remote(both, both, rs_sem.at[l, 1, 0], rs_sem.at[l, 1, 1], xy_peer(other))

    def z_piece(l, other, lanes):
        part = zb.at[l, z, :, lanes]
        return remote(part, part, z_sem.at[l, 0, 0], z_sem.at[l, 0, 1], z_peer(other))

    def z_mean(l, other):
        part = zm.at[l, z]
        return remote(part, part, z_sem.at[l, 1, 0], z_sem.at[l, 1, 1], z_peer(other))

    def ag_piece(l, n, lanes):
        part = ga.at[l, core, k, :, lanes]
        return remote(
            part, part, ag_send.at[l], ag_recv.at[l, n // 4], xy_peer(xy_others[n])
        )

    def fw_piece(l, slot, lanes):
        part = ga.at[l, core, slot, :, lanes]
        return remote(part, part, fw_sem.at[l, 0], fw_sem.at[l, 1], partner)

    def local_gram(l, values):
        mean = jnp.sum(values, axis=0, keepdims=True) * (1.0 / OWN)
        means[l, 2 * k + core] = mean
        cen = (values - mean).astype(BF16)
        pair_mean(l).start()
        gram = lax.dot_general(cen, cen, (((0,), (0,)), ((), ())), preferred_element_type=F32)
        for i in range(4):
            for d in range(3 if i < 2 else 2):
                j = (i + d) % 4
                block = gram[128 * i : 128 * i + 128, 128 * j : 128 * j + 128].astype(BF16)
                s0[l, i // 2, (i % 2) * 8 : (i % 2) * 8 + 8, :, 128 * d : 128 * d + 128] = (
                    block.reshape(8, 16, 128)
                )
        by_core(1 - core, lambda lanes: pair_piece(l, lanes).start())

    def rs_start(l):
        pair_mean_in(l).wait_recv()
        for other in xy_others:
            rs_mean(l, other).start()
        by_core(core, lambda lanes: wait_all(r0.at[l, :, :, lanes], pair_recv.at[l, 0]))
        tsum[l] = (s0[l, core].astype(F32) + r0[l].astype(F32)).astype(BF16)
        r1[l, k] = tsum[l, k]

        def send(lanes):
            for other in xy_others:
                rs_piece(l, other, lanes).start()

        by_core(core, send)

    def spread(rows):
        n = rows.shape[0]
        mean = jnp.sum(rows, axis=0, keepdims=True) * (1.0 / n)
        off = rows - mean
        dxs[0:n, 0:C1] = off
        dxs[0:n, C1:] = off[:, 0:256]
        lane = lax.broadcasted_iota(jnp.int32, (16, C1), 1)
        sub = lax.broadcasted_iota(jnp.int32, (16, C1), 0)
        pick = jnp.where(lane == strip * 16 + sub, 1.0, 0.0).astype(F32)
        left = lax.dot_general(
            pick, off, (((1,), (1,)), ((), ())), precision=HIGHEST, preferred_element_type=F32
        )
        right = dxs[0:n, pl.ds(pl.multiple_of((strip // 8) * 128, 128), 384)]
        return mean, jnp.dot(left, right, precision=HIGHEST, preferred_element_type=F32)

    def plane_done(l):
        wait_all(means.at[l, pl.ds(0, 30)], rs_sem.at[l, 1, 1])
        mean, extra = spread(means[l].reshape(32, C1))
        zm[l, z] = mean
        by_core(
            core,
            lambda lanes: wait_all(r1.at[l, pl.ds(0, 15), :, lanes], rs_sem.at[l, 0, 1]),
        )
        for other in z_others:
            z_mean(l, other).start()
        total = jnp.sum(r1[l].astype(F32), axis=0) + float(OWN) * extra
        zb[l, z] = total.astype(Z_TYPE)

        def send(lanes):
            for other in z_others:
                z_piece(l, other, lanes).start()

        by_core(core, send)

    def z_done(l):
        wait_all(zm.at[l, pl.ds(0, 7)], z_sem.at[l, 1, 1])
        mean, extra = spread(zm[l].reshape(8, C1))
        by_core(
            core, lambda lanes: wait_all(zb.at[l, pl.ds(0, 7), :, lanes], z_sem.at[l, 0, 1])
        )
        total = jnp.sum(zb[l].astype(F32), axis=0) + float(32 * OWN) * extra
        ga[l, core, k] = (total * (1.0 / CELLS)).astype(BF16)

        def send(lanes):
            for n in range(15):
                ag_piece(l, n, lanes).start()
            fw_piece(l, k, lanes).start()

        by_core(core, send)
        return mean

    def gathered(l):
        def forward(lanes):
            for n in range(15):
                if n % 4 == 0:
                    wait_all(
                        ga.at[l, core, pl.ds(0, min(4, 15 - n)), :, lanes], ag_recv.at[l, n // 4]
                    )
                fw_piece(l, xy_from[n], lanes).start()

        by_core(core, forward)

    def forwarded(l):
        by_core(1 - core, lambda lanes: wait_all(ga.at[l, 1 - core, :, :, lanes], fw_sem.at[l, 1]))

    def mismatch(l):
        def put(i, j, block):
            block = block - ts[l, 128 * i : 128 * i + 128, 128 * j : 128 * j + 128]
            top = block.astype(BF16)
            sh[l, 128 * i : 128 * i + 128, 128 * j : 128 * j + 128] = top
            sl[l, 128 * i : 128 * i + 128, 128 * j : 128 * j + 128] = (
                block - top.astype(F32)
            ).astype(BF16)

        for i in range(4):
            for d in range(3 if i < 2 else 2):
                block = ga[l, i // 2, (i % 2) * 8 : (i % 2) * 8 + 8, :, 128 * d : 128 * d + 128]
                block = block.astype(F32).reshape(128, 128)
                put(i, (i + d) % 4, block)
                if d > 0:
                    put((i + d) % 4, i, block.T)

    local_gram(0, flat(act1[3:11, 8:72, :]))

    loads[3].wait()

    def conv2_main(i, carry):
        total = None
        for a in range(3):
            part = dot_nn(flat(fsm[pl.ds(4 * i + a, 4)]), w2[a])
            total = part if total is None else total + part
        act2m[pl.ds(4 * i, 4)] = gelu_value(total).reshape(4, 64, C1)
        return carry

    conv2_main(0, 0)
    rs_start(0)
    conv2_main(1, 0)
    local_gram(1, flat(act2m[...]))

    wait_all(pad.at[pl.ds(0, 5), pl.ds(0, 8)], halo_sem.at[2])
    clear_pad(0, 14, ((0, 2), (14, 2)))
    rows_loop(0, 2, shift_pool, 2)
    rows_loop(14, 16, shift_pool, 2)

    conv1_from([(0, 2, 0, W), (12, 2, 0, W)])
    rs_start(1)

    def finish_first(r, carry):
        value, slope = gelu_both(pre1[r])
        act1[r] = value
        sl1[r] = slope
        return carry

    def shift_first_all(r, carry):
        row = act1[r]
        for b in range(3):
            fs[r, :, b * C1 : (b + 1) * C1] = ahead(row, b - 1).astype(BF16)
        return carry

    def conv2_all(i, carry):
        total = None
        for a in range(3):
            part = dot_nn(flat(fs[pl.ds(3 * i + a, 3)]), w2[a])
            total = part if total is None else total + part
        value, slope = gelu_both(total)
        act2[pl.ds(3 * i, 3)] = value.reshape(3, W, C1)
        sl2[pl.ds(3 * i, 3)] = slope.reshape(3, W, C1)
        return carry

    rows_loop(0, 14, finish_first, 2)
    clear_edges(act1, 0, 14, 3)
    clear_edges(sl1, 2, 10, 1)
    plane_done(0)
    rows_loop(0, 14, shift_first_all, 7)
    conv2_all(0, 0)
    plane_done(1)
    conv2_all(1, 0)
    mean_first = z_done(0)
    conv2_all(2, 0)
    mean_second = z_done(1)
    conv2_all(3, 0)
    clear_edges(sl2, 0, 12, 2)

    def centre(source, high, low, mean, shift):
        def step(r, carry):
            cen = source[r + shift] - mean
            top = cen.astype(BF16)
            high[r] = top
            low[r] = (cen - top.astype(F32)).astype(BF16)
            return carry

        return step

    rows_loop(0, 10, centre(act1, ch1, cl1, mean_first, 2), 5)
    rows_loop(0, 12, centre(act2, ch2, cl2, mean_second, 0), 4)

    def push(l, high, low, first, rows):
        top = flat(high[pl.ds(first, rows)])
        rest = flat(low[pl.ds(first, rows)])
        return dot_nn(top, sh[l]) + dot_nn(rest, sh[l]) + dot_nn(top, sl[l])

    def push_first(i, carry):
        flow1[pl.ds(5 * i, 5)] = push(0, ch1, cl1, 5 * i, 5).reshape(5, W, C1)
        return carry

    gathered(0)
    wait_all(pad.at[pl.ds(0, 12), pl.ds(0, 8)], halo_sem.at[0])
    for l in range(2):
        by_core(1 - core, lambda lanes: wait_all(r0.at[l, :, :, lanes], pair_send.at[l, 0]))
        pair_mean(l).wait_send()

        def sent(lanes):
            wait_all(r1.at[l, pl.ds(0, 15), :, lanes], rs_sem.at[l, 0, 0])
            wait_all(zb.at[l, pl.ds(0, 7), :, lanes], z_sem.at[l, 0, 0])

        by_core(core, sent)
        wait_all(means.at[l, pl.ds(0, 30)], rs_sem.at[l, 1, 0])
        wait_all(zm.at[l, pl.ds(0, 7)], z_sem.at[l, 1, 0])
    forwarded(0)
    mismatch(0)
    push_first(0, 0)
    gathered(1)
    push_first(1, 0)
    forwarded(1)

    mismatch(1)

    def back2(i, carry):
        grad = push(1, ch2, cl2, 4 * i, 4) * flat(sl2[pl.ds(4 * i, 4)])
        for b in range(3):
            gs2[pl.ds(4 * i, 4), :, b * C1 : (b + 1) * C1] = (
                ahead(grad, 1 - b).astype(BF16).reshape(4, W, C1)
            )
        return carry

    lax.fori_loop(0, 3, back2, 0, unroll=True)

    def back1(i, carry):
        flow = flat(flow1[pl.ds(5 * i, 5)])
        for a in range(3):
            for b in range(3):
                flow = flow + dot_nt(
                    flat(gs2[pl.ds(5 * i + 2 - a, 5), :, b * C1 : (b + 1) * C1]),
                    w2[a, b * C1 : (b + 1) * C1, :],
                )
        grad = flow * flat(sl1[pl.ds(5 * i + 2, 5)])
        for b in range(3):
            gs1[pl.ds(5 * i, 5), :, b * C1 : (b + 1) * C1] = (
                ahead(grad, 1 - b).reshape(5, W, C1)[:, 8:72].astype(BF16)
            )
        return carry

    lax.fori_loop(0, 2, back1, 0, unroll=True)

    for l in range(2):

        def gone(lanes):
            wait_all(ga.at[l, core, pl.ds(0, 15), :, lanes], ag_send.at[l])
            wait_all(ga.at[l, core, :, :, lanes], fw_sem.at[l, 0])

        by_core(core, gone)

    def back0(i, carry):
        total = None
        for a in range(3):
            for b in range(3):
                part = dot_nt(
                    flat(gs1[pl.ds(4 * i + 2 - a, 4), :, b * C1 : (b + 1) * C1]),
                    w1[a, b * C0 : (b + 1) * C0, :],
                )
                total = part if total is None else total + part
        out[pl.ds(4 * i, 4)] = total.reshape(4, 64, C0)
        return carry

    lax.fori_loop(0, 2, back0, 0, unroll=True)


def local(pool_input, weight_first, weight_second, targets):
    v = pltpu.VMEM
    dma = pltpu.SemaphoreType.DMA
    scratch = [
        v((8, 64, C0), F32),
        v((3, 3 * C0, C1), BF16),
        v((3, 3 * C1, C1), BF16),
        v((2, C1, C1), F32),
        v((2, C1, C1), F32),
        v((16, 10, 8, C0), BF16),
        v((16, W, 3 * C0), BF16),
        v((14, W, C1), F32),
        v((14, W, C1), F32),
        v((14, W, C1), F32),
        v((10, 64, 3 * C1), BF16),
        v((14, W, 3 * C1), BF16),
        v((8, 64, C1), F32),
        v((12, W, C1), F32),
        v((12, W, C1), F32),
        v((10, W, C1), BF16),
        v((10, W, C1), BF16),
        v((12, W, C1), BF16),
        v((12, W, C1), BF16),
        v((2, 2, 16, 16, 384), BF16),
        v((2, 16, 16, 384), BF16),
        v((2, 16, 16, 384), BF16),
        v((2, 16, 16, 384), BF16),
        v((2, 32, 1, C1), F32),
        v((32, C1 + 256), F32),
        v((2, 8, 16, 384), Z_TYPE),
        v((2, 8, 1, C1), F32),
        v((2, 2, 16, 16, 384), BF16),
        v((2, C1, C1), BF16),
        v((2, C1, C1), BF16),
        dma((4,)),
        dma((3,)),
        dma((2, 2)),
        dma((2, 2)),
        dma((2, 2, 2)),
        dma((2, 2, 2)),
        dma((2,)),
        dma((2, 4)),
        dma((2, 2)),
    ]
    return pl.pallas_call(
        kernel,
        out_shape=pltpu.VMEM((8, 64, C0), F32),
        in_specs=[pl.BlockSpec(memory_space=pltpu.HBM)] * 4,
        out_specs=pl.BlockSpec(memory_space=pltpu.VMEM),
        scratch_shapes=scratch,
        compiler_params=pltpu.CompilerParams(
            collective_id=0, has_side_effects=True, vmem_limit_bytes=67043328 - 768 * 1024
        ),
        name="style_grad",
    )(
        pool_input,
        weight_first.reshape(3, 3 * C0, C1),
        weight_second.reshape(3, 3 * C1, C1),
        targets,
    )


def solution(mesh):
    return jax.shard_map(
        local,
        mesh=mesh,
        in_specs=(P("grp", "tile", None), P(), P(), P()),
        out_specs=P("grp", "tile", None),
        check_vma=False,
    )
```

```python
import functools

import jax
import jax.numpy as jnp
from jax import lax
from jax.experimental import pallas as pl
from jax.experimental.pallas import tpu as pltpu
from jax.sharding import PartitionSpec as P

GELU_SCALE = 0.7978845608
GELU_CUBIC = 0.044715
F32 = jnp.float32
BF16 = jnp.bfloat16
HIGHEST = lax.Precision.HIGHEST
MESH = pl.DeviceIdType.MESH
Z_TYPE = BF16
CELLS = 64 * 2048
OWN = 512
C0, C1 = 256, 512
W = 80


def gelu_value(z):
    return 0.5 * z * (1.0 + jnp.tanh(GELU_SCALE * (z + GELU_CUBIC * (z * z * z))))


def gelu_both(z):
    square = z * z
    hyper = jnp.tanh(GELU_SCALE * (z + GELU_CUBIC * (square * z)))
    half = 0.5 * (1.0 + hyper)
    slope = half + 0.5 * z * (1.0 - hyper * hyper) * GELU_SCALE * (1.0 + 3.0 * GELU_CUBIC * square)
    return z * half, slope


def flat(block):
    return block.reshape(block.shape[0] * block.shape[1], block.shape[2])


def dot_nn(left, right):
    return jnp.dot(left, right, preferred_element_type=F32)


def dot_nt(left, right):
    return lax.dot_general(left, right, (((1,), (1,)), ((), ())), preferred_element_type=F32)


def ahead(x, step):
    return x if step == 0 else pltpu.roll(x, (-step) % x.shape[0], 0)


def kernel(
    pool_hbm, w1_hbm, w2_hbm, tg_hbm, out,
    pool, w1, w2, tg, ts, pad, xs, pre1, act1, sl1, fsm, fs, act2m, act2, sl2,
    ch1, cl1, ch2, cl2, s0, r0, tsum, r1, means, dxs, zb, zm, ga, sh, sl,
    local_sem, halo_sem, pair_send, pair_recv, rs_sem, z_sem, ag_send, ag_recv, fw_sem,
):
    gs1, gs2, flow1 = fsm, fs, pre1
    g = lax.axis_index("grp")
    t = lax.axis_index("tile")
    core = lax.rem(t, 2)
    x = lax.rem(t // 2, 2) * 2 + g // 4
    y = lax.rem(g, 4)
    z = t // 4
    k = x * 4 + y
    strip = core * 16 + k

    def device(x_to, y_to, z_to, core_to):
        return (lax.rem(x_to, 2) * 4 + y_to, z_to * 4 + (x_to // 2) * 2 + core_to)

    partner = device(x, y, z, 1 - core)

    def xy_peer(other):
        return device(other // 4, lax.rem(other, 4), z, core)

    def z_peer(other):
        return device(x, y, other, core)

    xy_steps = sorted(
        ((i, j) for i in range(4) for j in range(4) if (i, j) != (0, 0)),
        key=lambda s: -(min(s[0], 4 - s[0]) + min(s[1], 4 - s[1])),
    )
    xy_others = [lax.rem(x + i, 4) * 4 + lax.rem(y + j, 4) for i, j in xy_steps]
    xy_from = [lax.rem(x + 4 - i, 4) * 4 + lax.rem(y + 4 - j, 4) for i, j in xy_steps]
    z_others = [lax.rem(z + i, 8) for i in (4, 3, 5, 2, 6, 1, 7)]
    sides = [(i, j) for i in (-1, 1) for j in (-1, 1, 0)] + [(0, -1), (0, 1)]

    def side_peer(i, j):
        return (lax.rem(g + i + 8, 8), lax.rem(t + j + 32, 32))

    loads = [
        pltpu.make_async_copy(source, target, local_sem.at[i])
        for i, (source, target) in enumerate(
            (
                (pool_hbm, pool),
                (w1_hbm.at[0], w1.at[0]),
                (w1_hbm.at[1], w1.at[1]),
                (w1_hbm.at[2], w1.at[2]),
                (tg_hbm, tg),
                (w2_hbm, w2),
            )
        )
    ]
    for load in loads[:4]:
        load.start()
    barrier = pltpu.get_barrier_semaphore()

    def greet(who):
        pl.semaphore_signal(barrier, inc=1, device_id=who, device_id_type=MESH)

    for i, j in sides:
        greet(side_peer(i, j))
    for other in xy_others:
        greet(xy_peer(other))
    for other in z_others:
        greet(z_peer(other))
    greet(partner)
    loads[0].wait()
    pad[4:12, 1:9] = pool[...].astype(BF16).reshape(8, 8, 8, C0)
    def rows_loop(first, last, step, at_once):
        def some(i, carry):
            for n in range(at_once):
                step(first + i * at_once + n, carry)
            return carry

        times = (last - first) // at_once
        lax.fori_loop(0, times, some, 0, unroll=times == 1)

    def conv1_from(pieces, weights=None):
        total = None
        for a in range(3):
            if weights is not None:
                weights[a].wait()
            left = [flat(xs[pl.ds(row + a, rows), col : col + cols]) for row, rows, col, cols in pieces]
            part = dot_nn(jnp.concatenate(left, axis=0) if len(left) > 1 else left[0], w1[a])
            total = part if total is None else total + part
        at = 0
        for row, rows, col, cols in pieces:
            n = rows * cols
            pre1[pl.ds(row, rows), col : col + cols] = total[at : at + n].reshape(rows, cols, C1)
            at += n

    def shift_inner(r, carry):
        row = pool[r - 4].astype(BF16).astype(F32)
        for b in range(3):
            xs[r, 16:64, b * C0 : (b + 1) * C0] = ahead(row, b - 1)[8:56].astype(BF16)
        return carry

    def gelu_inner(r, carry):
        act1[r, 16:64] = gelu_value(pre1[r, 16:64])
        return carry

    rows_loop(4, 12, shift_inner, 4)
    conv1_from([(4, 6, 16, 48)], loads[1:4])
    for load in loads[4:]:
        load.start()
    rows_loop(4, 10, gelu_inner, 3)
    pl.semaphore_wait(barrier, 31)

    cols_from = {1: (8, 1), 0: (1, 8), -1: (1, 1)}
    cols_to = {1: (0, 1), 0: (1, 8), -1: (9, 1)}

    def halo(i, j, row_from, row_to, rows, arrival):
        (fc, nc), (tc, _) = cols_from[j], cols_to[j]
        return pltpu.make_async_remote_copy(
            src_ref=pad.at[pl.ds(row_from, rows), pl.ds(fc, nc)],
            dst_ref=pad.at[pl.ds(row_to, rows), pl.ds(tc, nc)],
            send_sem=halo_sem.at[0],
            recv_sem=halo_sem.at[arrival],
            device_id=side_peer(i, j),
            device_id_type=MESH,
        )

    near_rows = {1: (10, 2, 2), 0: (4, 4, 8), -1: (4, 12, 2)}
    far_rows = {1: (8, 0, 2), -1: (6, 14, 2)}
    near = [halo(i, j, *near_rows[i], 1) for i, j in sides]
    far = [halo(i, j, *far_rows[i], 2) for i, j in sides if i != 0]
    for copy in near:
        copy.start()

    def wait_all(part, sem):
        pltpu.make_async_copy(part, part, sem).wait()

    loads[4].wait()
    for l in range(2):
        whole = tg[l]
        ts[l] = (whole + whole.T) * 0.5
    wait_all(pad.at[pl.ds(0, 7), pl.ds(0, 8)], halo_sem.at[1])
    for copy in far:
        copy.start()

    def on_edges(top, bottom, left, right):
        pl.when(g == 0)(top)
        pl.when(g == 7)(bottom)
        pl.when(t == 0)(left)
        pl.when(t == 31)(right)

    def clear_pad(up, down, blocks):
        def zero(first, rows, col, cols):
            pad[first : first + rows, col : col + cols] = jnp.zeros((rows, cols, 8, C0), BF16)

        def column(col):
            for first, rows in blocks:
                zero(first, rows, col, 1)

        on_edges(
            lambda: zero(up, 2, 0, 10),
            lambda: zero(down, 2, 0, 10),
            lambda: column(0),
            lambda: column(9),
        )

    def clear_edges(ref, first, rows, depth):
        def zero(row, n, col, cols):
            ref[row : row + n, col : col + cols] = jnp.zeros((n, cols, ref.shape[2]), ref.dtype)

        on_edges(
            lambda: zero(first, depth, 0, W),
            lambda: zero(first + rows - depth, depth, 0, W),
            lambda: zero(first, rows, 0, 8),
            lambda: zero(first, rows, W - 8, 8),
        )

    clear_pad(2, 12, ((2, 12),))

    def shift_pool(r, carry):
        row = pad[r].astype(F32).reshape(W, C0)
        for b in range(3):
            xs[r, :, b * C0 : (b + 1) * C0] = ahead(row, b - 1).astype(BF16)
        return carry

    def gelu_row(r, carry):
        act1[r] = gelu_value(pre1[r])
        return carry

    def gelu_sides(r, carry):
        for col in (0, 64):
            act1[r, col : col + 16] = gelu_value(pre1[r, col : col + 16])
        return carry

    rows_loop(2, 14, shift_pool, 4)
    conv1_from([(2, 2, 0, W), (10, 2, 0, W)])
    rows_loop(2, 4, gelu_row, 2)
    rows_loop(10, 12, gelu_row, 2)
    conv1_from([(4, 6, 0, 16), (4, 6, 64, 16)])
    rows_loop(4, 10, gelu_sides, 6)
    clear_edges(act1, 2, 10, 1)

    def shift_first(r, carry):
        row = act1[r + 2]
        for b in range(3):
            fsm[r, :, b * C1 : (b + 1) * C1] = ahead(row, b - 1)[8:72].astype(BF16)
        return carry

    rows_loop(0, 10, shift_first, 5)

    def remote(source, target, send, recv, who):
        return pltpu.make_async_remote_copy(
            src_ref=source, dst_ref=target, send_sem=send, recv_sem=recv,
            device_id=who, device_id_type=MESH,
        )

    def by_core(who, act):
        pl.when(who == 0)(lambda: act(pl.ds(0, 384)))
        pl.when(who == 1)(lambda: act(pl.ds(0, 256)))

    def pair_piece(l, lanes):
        return remote(
            s0.at[l, 1 - core, :, :, lanes],
            r0.at[l, :, :, lanes],
            pair_send.at[l, 0],
            pair_recv.at[l, 0],
            partner,
        )

    def pair_mean(l):
        own = means.at[l, 2 * k + core]
        return remote(own, own, pair_send.at[l, 1], pair_recv.at[l, 1], partner)

    def pair_mean_in(l):
        other = means.at[l, 2 * k + 1 - core]
        return remote(other, other, pair_send.at[l, 1], pair_recv.at[l, 1], partner)

    def rs_piece(l, other, lanes):
        return remote(
            tsum.at[l, other, :, lanes], r1.at[l, k, :, lanes], rs_sem.at[l, 0, 0], rs_sem.at[l, 0, 1], xy_peer(other)
        )

    def rs_mean(l, other):
        both = means.at[l, pl.ds(2 * k, 2)]
        return remote(both, both, rs_sem.at[l, 1, 0], rs_sem.at[l, 1, 1], xy_peer(other))

    def z_piece(l, other, lanes):
        part = zb.at[l, z, :, lanes]
        return remote(part, part, z_sem.at[l, 0, 0], z_sem.at[l, 0, 1], z_peer(other))

    def z_mean(l, other):
        part = zm.at[l, z]
        return remote(part, part, z_sem.at[l, 1, 0], z_sem.at[l, 1, 1], z_peer(other))

    def ag_piece(l, n, lanes):
        part = ga.at[l, core, k, :, lanes]
        return remote(
            part, part, ag_send.at[l], ag_recv.at[l, n // 4], xy_peer(xy_others[n])
        )

    def fw_piece(l, slot, lanes):
        part = ga.at[l, core, slot, :, lanes]
        return remote(part, part, fw_sem.at[l, 0], fw_sem.at[l, 1], partner)

    def local_gram(l, values):
        mean = jnp.sum(values, axis=0, keepdims=True) * (1.0 / OWN)
        means[l, 2 * k + core] = mean
        cen = (values - mean).astype(BF16)
        pair_mean(l).start()
        gram = lax.dot_general(cen, cen, (((0,), (0,)), ((), ())), preferred_element_type=F32)
        for i in range(4):
            for d in range(3 if i < 2 else 2):
                j = (i + d) % 4
                block = gram[128 * i : 128 * i + 128, 128 * j : 128 * j + 128].astype(BF16)
                s0[l, i // 2, (i % 2) * 8 : (i % 2) * 8 + 8, :, 128 * d : 128 * d + 128] = (
                    block.reshape(8, 16, 128)
                )
        by_core(1 - core, lambda lanes: pair_piece(l, lanes).start())

    def rs_start(l):
        pair_mean_in(l).wait_recv()
        for other in xy_others:
            rs_mean(l, other).start()
        by_core(core, lambda lanes: wait_all(r0.at[l, :, :, lanes], pair_recv.at[l, 0]))
        tsum[l] = (s0[l, core].astype(F32) + r0[l].astype(F32)).astype(BF16)
        r1[l, k] = tsum[l, k]

        def send(lanes):
            for other in xy_others:
                rs_piece(l, other, lanes).start()

        by_core(core, send)

    def spread(rows):
        n = rows.shape[0]
        mean = jnp.sum(rows, axis=0, keepdims=True) * (1.0 / n)
        off = rows - mean
        dxs[0:n, 0:C1] = off
        dxs[0:n, C1:] = off[:, 0:256]
        lane = lax.broadcasted_iota(jnp.int32, (16, C1), 1)
        sub = lax.broadcasted_iota(jnp.int32, (16, C1), 0)
        pick = jnp.where(lane == strip * 16 + sub, 1.0, 0.0).astype(F32)
        left = lax.dot_general(
            pick, off, (((1,), (1,)), ((), ())), precision=HIGHEST, preferred_element_type=F32
        )
        right = dxs[0:n, pl.ds(pl.multiple_of((strip // 8) * 128, 128), 384)]
        return mean, jnp.dot(left, right, precision=HIGHEST, preferred_element_type=F32)

    def plane_done(l):
        wait_all(means.at[l, pl.ds(0, 30)], rs_sem.at[l, 1, 1])
        mean, extra = spread(means[l].reshape(32, C1))
        zm[l, z] = mean
        by_core(
            core,
            lambda lanes: wait_all(r1.at[l, pl.ds(0, 15), :, lanes], rs_sem.at[l, 0, 1]),
        )
        for other in z_others:
            z_mean(l, other).start()
        total = jnp.sum(r1[l].astype(F32), axis=0) + float(OWN) * extra
        zb[l, z] = total.astype(Z_TYPE)

        def send(lanes):
            for other in z_others:
                z_piece(l, other, lanes).start()

        by_core(core, send)

    def z_done(l):
        wait_all(zm.at[l, pl.ds(0, 7)], z_sem.at[l, 1, 1])
        mean, extra = spread(zm[l].reshape(8, C1))
        by_core(
            core, lambda lanes: wait_all(zb.at[l, pl.ds(0, 7), :, lanes], z_sem.at[l, 0, 1])
        )
        total = jnp.sum(zb[l].astype(F32), axis=0) + float(32 * OWN) * extra
        ga[l, core, k] = (total * (1.0 / CELLS)).astype(BF16)

        def send(lanes):
            for n in range(15):
                ag_piece(l, n, lanes).start()
            fw_piece(l, k, lanes).start()

        by_core(core, send)
        return mean

    def gathered(l):
        def forward(lanes):
            for n in range(15):
                if n % 4 == 0:
                    wait_all(
                        ga.at[l, core, pl.ds(0, min(4, 15 - n)), :, lanes], ag_recv.at[l, n // 4]
                    )
                fw_piece(l, xy_from[n], lanes).start()

        by_core(core, forward)

    def forwarded(l):
        by_core(1 - core, lambda lanes: wait_all(ga.at[l, 1 - core, :, :, lanes], fw_sem.at[l, 1]))

    def mismatch(l):
        def put(i, j, block):
            block = block - ts[l, 128 * i : 128 * i + 128, 128 * j : 128 * j + 128]
            top = block.astype(BF16)
            sh[l, 128 * i : 128 * i + 128, 128 * j : 128 * j + 128] = top
            sl[l, 128 * i : 128 * i + 128, 128 * j : 128 * j + 128] = (
                block - top.astype(F32)
            ).astype(BF16)

        for i in range(4):
            for d in range(3 if i < 2 else 2):
                block = ga[l, i // 2, (i % 2) * 8 : (i % 2) * 8 + 8, :, 128 * d : 128 * d + 128]
                block = block.astype(F32).reshape(128, 128)
                put(i, (i + d) % 4, block)
                if d > 0:
                    put((i + d) % 4, i, block.T)

    local_gram(0, flat(act1[3:11, 8:72, :]))

    loads[5].wait()

    def conv2_main(i, carry):
        total = None
        for a in range(3):
            part = dot_nn(flat(fsm[pl.ds(4 * i + a, 4)]), w2[a])
            total = part if total is None else total + part
        act2m[pl.ds(4 * i, 4)] = gelu_value(total).reshape(4, 64, C1)
        return carry

    conv2_main(0, 0)
    rs_start(0)
    conv2_main(1, 0)
    local_gram(1, flat(act2m[...]))

    wait_all(pad.at[pl.ds(0, 5), pl.ds(0, 8)], halo_sem.at[2])
    clear_pad(0, 14, ((0, 2), (14, 2)))
    rows_loop(0, 2, shift_pool, 2)
    rows_loop(14, 16, shift_pool, 2)

    conv1_from([(0, 2, 0, W), (12, 2, 0, W)])
    rs_start(1)

    def finish_first(r, carry):
        value, slope = gelu_both(pre1[r])
        act1[r] = value
        sl1[r] = slope
        return carry

    def shift_first_all(r, carry):
        row = act1[r]
        for b in range(3):
            fs[r, :, b * C1 : (b + 1) * C1] = ahead(row, b - 1).astype(BF16)
        return carry

    def conv2_all(i, carry):
        total = None
        for a in range(3):
            part = dot_nn(flat(fs[pl.ds(3 * i + a, 3)]), w2[a])
            total = part if total is None else total + part
        value, slope = gelu_both(total)
        act2[pl.ds(3 * i, 3)] = value.reshape(3, W, C1)
        sl2[pl.ds(3 * i, 3)] = slope.reshape(3, W, C1)
        return carry

    rows_loop(0, 14, finish_first, 2)
    clear_edges(act1, 0, 14, 3)
    clear_edges(sl1, 2, 10, 1)
    plane_done(0)
    rows_loop(0, 14, shift_first_all, 7)
    conv2_all(0, 0)
    plane_done(1)
    conv2_all(1, 0)
    mean_first = z_done(0)
    conv2_all(2, 0)
    mean_second = z_done(1)
    conv2_all(3, 0)
    clear_edges(sl2, 0, 12, 2)

    def centre(source, high, low, mean, shift):
        def step(r, carry):
            cen = source[r + shift] - mean
            top = cen.astype(BF16)
            high[r] = top
            low[r] = (cen - top.astype(F32)).astype(BF16)
            return carry

        return step

    rows_loop(0, 10, centre(act1, ch1, cl1, mean_first, 2), 5)
    rows_loop(0, 12, centre(act2, ch2, cl2, mean_second, 0), 4)

    def push(l, high, low, first, rows):
        top = flat(high[pl.ds(first, rows)])
        rest = flat(low[pl.ds(first, rows)])
        return dot_nn(top, sh[l]) + dot_nn(rest, sh[l]) + dot_nn(top, sl[l])

    def push_first(i, carry):
        flow1[pl.ds(5 * i, 5)] = push(0, ch1, cl1, 5 * i, 5).reshape(5, W, C1)
        return carry

    gathered(0)
    wait_all(pad.at[pl.ds(0, 12), pl.ds(0, 8)], halo_sem.at[0])
    for l in range(2):
        by_core(1 - core, lambda lanes: wait_all(r0.at[l, :, :, lanes], pair_send.at[l, 0]))
        pair_mean(l).wait_send()

        def sent(lanes):
            wait_all(r1.at[l, pl.ds(0, 15), :, lanes], rs_sem.at[l, 0, 0])
            wait_all(zb.at[l, pl.ds(0, 7), :, lanes], z_sem.at[l, 0, 0])

        by_core(core, sent)
        wait_all(means.at[l, pl.ds(0, 30)], rs_sem.at[l, 1, 0])
        wait_all(zm.at[l, pl.ds(0, 7)], z_sem.at[l, 1, 0])
    forwarded(0)
    mismatch(0)
    push_first(0, 0)
    gathered(1)
    push_first(1, 0)
    forwarded(1)

    mismatch(1)

    def back2(i, carry):
        grad = push(1, ch2, cl2, 4 * i, 4) * flat(sl2[pl.ds(4 * i, 4)])
        for b in range(3):
            gs2[pl.ds(4 * i, 4), :, b * C1 : (b + 1) * C1] = (
                ahead(grad, 1 - b).astype(BF16).reshape(4, W, C1)
            )
        return carry

    lax.fori_loop(0, 3, back2, 0, unroll=True)

    def back1(i, carry):
        flow = flat(flow1[pl.ds(5 * i, 5)])
        for a in range(3):
            for b in range(3):
                flow = flow + dot_nt(
                    flat(gs2[pl.ds(5 * i + 2 - a, 5), :, b * C1 : (b + 1) * C1]),
                    w2[a, b * C1 : (b + 1) * C1, :],
                )
        grad = flow * flat(sl1[pl.ds(5 * i + 2, 5)])
        for b in range(3):
            gs1[pl.ds(5 * i, 5), :, b * C1 : (b + 1) * C1] = (
                ahead(grad, 1 - b).reshape(5, W, C1)[:, 8:72].astype(BF16)
            )
        return carry

    lax.fori_loop(0, 2, back1, 0, unroll=True)

    for l in range(2):

        def gone(lanes):
            wait_all(ga.at[l, core, pl.ds(0, 15), :, lanes], ag_send.at[l])
            wait_all(ga.at[l, core, :, :, lanes], fw_sem.at[l, 0])

        by_core(core, gone)

    def back0(i, carry):
        total = None
        for a in range(3):
            for b in range(3):
                part = dot_nt(
                    flat(gs1[pl.ds(4 * i + 2 - a, 4), :, b * C1 : (b + 1) * C1]),
                    w1[a, b * C0 : (b + 1) * C0, :],
                )
                total = part if total is None else total + part
        out[pl.ds(4 * i, 4)] = total.reshape(4, 64, C0)
        return carry

    lax.fori_loop(0, 2, back0, 0, unroll=True)


def local(pool_input, weight_first, weight_second, targets):
    v = pltpu.VMEM
    dma = pltpu.SemaphoreType.DMA
    scratch = [
        v((8, 64, C0), F32),
        v((3, 3 * C0, C1), BF16),
        v((3, 3 * C1, C1), BF16),
        v((2, C1, C1), F32),
        v((2, C1, C1), F32),
        v((16, 10, 8, C0), BF16),
        v((16, W, 3 * C0), BF16),
        v((14, W, C1), F32),
        v((14, W, C1), F32),
        v((14, W, C1), F32),
        v((10, 64, 3 * C1), BF16),
        v((14, W, 3 * C1), BF16),
        v((8, 64, C1), F32),
        v((12, W, C1), F32),
        v((12, W, C1), F32),
        v((10, W, C1), BF16),
        v((10, W, C1), BF16),
        v((12, W, C1), BF16),
        v((12, W, C1), BF16),
        v((2, 2, 16, 16, 384), BF16),
        v((2, 16, 16, 384), BF16),
        v((2, 16, 16, 384), BF16),
        v((2, 16, 16, 384), BF16),
        v((2, 32, 1, C1), F32),
        v((32, C1 + 256), F32),
        v((2, 8, 16, 384), Z_TYPE),
        v((2, 8, 1, C1), F32),
        v((2, 2, 16, 16, 384), BF16),
        v((2, C1, C1), BF16),
        v((2, C1, C1), BF16),
        dma((6,)),
        dma((3,)),
        dma((2, 2)),
        dma((2, 2)),
        dma((2, 2, 2)),
        dma((2, 2, 2)),
        dma((2,)),
        dma((2, 4)),
        dma((2, 2)),
    ]
    return pl.pallas_call(
        kernel,
        out_shape=pltpu.VMEM((8, 64, C0), F32),
        in_specs=[pl.BlockSpec(memory_space=pltpu.HBM)] * 4,
        out_specs=pl.BlockSpec(memory_space=pltpu.VMEM),
        scratch_shapes=scratch,
        compiler_params=pltpu.CompilerParams(
            collective_id=0, has_side_effects=True, vmem_limit_bytes=67043328 - 768 * 1024
        ),
        name="style_grad",
    )(
        pool_input,
        weight_first.reshape(3, 3 * C0, C1),
        weight_second.reshape(3, 3 * C1, C1),
        targets,
    )


def solution(mesh):
    return jax.shard_map(
        local,
        mesh=mesh,
        in_specs=(P("grp", "tile", None), P(), P(), P()),
        out_specs=P("grp", "tile", None),
        check_vma=False,
    )
```

```python
import functools

import jax
import jax.numpy as jnp
from jax import lax
from jax.experimental import pallas as pl
from jax.experimental.pallas import tpu as pltpu
from jax.sharding import PartitionSpec as P

GELU_SCALE = 0.7978845608
GELU_CUBIC = 0.044715
F32 = jnp.float32
BF16 = jnp.bfloat16
HIGHEST = lax.Precision.HIGHEST
MESH = pl.DeviceIdType.MESH
Z_TYPE = BF16
CELLS = 64 * 2048
OWN = 512
C0, C1 = 256, 512
W = 80


def gelu_value(z):
    return 0.5 * z * (1.0 + jnp.tanh(GELU_SCALE * (z + GELU_CUBIC * (z * z * z))))


def gelu_both(z):
    square = z * z
    hyper = jnp.tanh(GELU_SCALE * (z + GELU_CUBIC * (square * z)))
    half = 0.5 * (1.0 + hyper)
    slope = half + 0.5 * z * (1.0 - hyper * hyper) * GELU_SCALE * (1.0 + 3.0 * GELU_CUBIC * square)
    return z * half, slope


def flat(block):
    return block.reshape(block.shape[0] * block.shape[1], block.shape[2])


def dot_nn(left, right):
    return jnp.dot(left, right, preferred_element_type=F32)


def dot_nt(left, right):
    return lax.dot_general(left, right, (((1,), (1,)), ((), ())), preferred_element_type=F32)


def ahead(x, step):
    return x if step == 0 else pltpu.roll(x, (-step) % x.shape[0], 0)


def kernel(
    pool_hbm, w1_hbm, w2_hbm, tg_hbm, out,
    pool, w1, w2, tg, ts, pad, xs, pre1, act1, sl1, fsm, fs, act2m, act2, sl2,
    ch1, cl1, ch2, cl2, s0, r0, tsum, r1, means, dxs, zb, zm, ga, sh, sl,
    local_sem, halo_sem, pair_send, pair_recv, rs_sem, z_sem, ag_send, ag_recv, fw_sem,
):
    gs1, gs2, flow1 = fsm, fs, pre1
    g = lax.axis_index("grp")
    t = lax.axis_index("tile")
    core = lax.rem(t, 2)
    x = lax.rem(t // 2, 2) * 2 + g // 4
    y = lax.rem(g, 4)
    z = t // 4
    k = x * 4 + y
    strip = core * 16 + k

    def device(x_to, y_to, z_to, core_to):
        return (lax.rem(x_to, 2) * 4 + y_to, z_to * 4 + (x_to // 2) * 2 + core_to)

    partner = device(x, y, z, 1 - core)

    def xy_peer(other):
        return device(other // 4, lax.rem(other, 4), z, core)

    def z_peer(other):
        return device(x, y, other, core)

    xy_steps = sorted(
        ((i, j) for i in range(4) for j in range(4) if (i, j) != (0, 0)),
        key=lambda s: -(min(s[0], 4 - s[0]) + min(s[1], 4 - s[1])),
    )
    xy_others = [lax.rem(x + i, 4) * 4 + lax.rem(y + j, 4) for i, j in xy_steps]
    xy_from = [lax.rem(x + 4 - i, 4) * 4 + lax.rem(y + 4 - j, 4) for i, j in xy_steps]
    z_others = [lax.rem(z + i, 8) for i in (4, 3, 5, 2, 6, 1, 7)]
    sides = [(i, j) for i in (-1, 1) for j in (-1, 1, 0)] + [(0, -1), (0, 1)]

    def side_peer(i, j):
        return (lax.rem(g + i + 8, 8), lax.rem(t + j + 32, 32))

    loads = [
        pltpu.make_async_copy(source, target, local_sem.at[i])
        for i, (source, target) in enumerate(
            (
                (pool_hbm, pool),
                (w1_hbm.at[0], w1.at[0]),
                (w1_hbm.at[1], w1.at[1]),
                (w1_hbm.at[2], w1.at[2]),
                (tg_hbm, tg),
                (w2_hbm, w2),
            )
        )
    ]
    for load in loads[:4]:
        load.start()
    barrier = pltpu.get_barrier_semaphore()

    def greet(who):
        pl.semaphore_signal(barrier, inc=1, device_id=who, device_id_type=MESH)

    for i, j in sides:
        greet(side_peer(i, j))
    for other in xy_others:
        greet(xy_peer(other))
    for other in z_others:
        greet(z_peer(other))
    greet(partner)
    loads[0].wait()
    pad[4:12, 1:9] = pool[...].astype(BF16).reshape(8, 8, 8, C0)
    def rows_loop(first, last, step, at_once):
        def some(i, carry):
            for n in range(at_once):
                step(first + i * at_once + n, carry)
            return carry

        times = (last - first) // at_once
        lax.fori_loop(0, times, some, 0, unroll=times == 1)

    def conv1_from(pieces, weights=None):
        total = None
        for a in range(3):
            if weights is not None:
                weights[a].wait()
            left = [flat(xs[pl.ds(row + a, rows), col : col + cols]) for row, rows, col, cols in pieces]
            part = dot_nn(jnp.concatenate(left, axis=0) if len(left) > 1 else left[0], w1[a])
            total = part if total is None else total + part
        at = 0
        for row, rows, col, cols in pieces:
            n = rows * cols
            pre1[pl.ds(row, rows), col : col + cols] = total[at : at + n].reshape(rows, cols, C1)
            at += n

    def shift_inner(r, carry):
        row = pool[r - 4].astype(BF16).astype(F32)
        for b in range(3):
            xs[r, 16:64, b * C0 : (b + 1) * C0] = ahead(row, b - 1)[8:56].astype(BF16)
        return carry

    def gelu_inner(r, carry):
        act1[r, 16:64] = gelu_value(pre1[r, 16:64])
        return carry

    rows_loop(4, 12, shift_inner, 4)
    conv1_from([(4, 6, 16, 48)], loads[1:4])
    for load in loads[4:]:
        load.start()
    rows_loop(4, 10, gelu_inner, 3)
    pl.semaphore_wait(barrier, 31)

    cols_from = {1: (8, 1), 0: (1, 8), -1: (1, 1)}
    cols_to = {1: (0, 1), 0: (1, 8), -1: (9, 1)}

    def halo(i, j, row_from, row_to, rows, arrival):
        (fc, nc), (tc, _) = cols_from[j], cols_to[j]
        return pltpu.make_async_remote_copy(
            src_ref=pad.at[pl.ds(row_from, rows), pl.ds(fc, nc)],
            dst_ref=pad.at[pl.ds(row_to, rows), pl.ds(tc, nc)],
            send_sem=halo_sem.at[0],
            recv_sem=halo_sem.at[arrival],
            device_id=side_peer(i, j),
            device_id_type=MESH,
        )

    near_rows = {1: (10, 2, 2), 0: (4, 4, 8), -1: (4, 12, 2)}
    far_rows = {1: (8, 0, 2), -1: (6, 14, 2)}
    near = [halo(i, j, *near_rows[i], 1) for i, j in sides]
    far = [halo(i, j, *far_rows[i], 2) for i, j in sides if i != 0]
    for copy in near:
        copy.start()

    def wait_all(part, sem):
        pltpu.make_async_copy(part, part, sem).wait()

    loads[4].wait()
    for l in range(2):
        whole = tg[l]
        ts[l] = (whole + whole.T) * 0.5
    wait_all(pad.at[pl.ds(0, 7), pl.ds(0, 8)], halo_sem.at[1])
    for copy in far:
        copy.start()

    def on_edges(top, bottom, left, right):
        pl.when(g == 0)(top)
        pl.when(g == 7)(bottom)
        pl.when(t == 0)(left)
        pl.when(t == 31)(right)

    def clear_pad(up, down, blocks):
        def zero(first, rows, col, cols):
            pad[first : first + rows, col : col + cols] = jnp.zeros((rows, cols, 8, C0), BF16)

        def column(col):
            for first, rows in blocks:
                zero(first, rows, col, 1)

        on_edges(
            lambda: zero(up, 2, 0, 10),
            lambda: zero(down, 2, 0, 10),
            lambda: column(0),
            lambda: column(9),
        )

    def clear_edges(ref, first, rows, depth):
        def zero(row, n, col, cols):
            ref[row : row + n, col : col + cols] = jnp.zeros((n, cols, ref.shape[2]), ref.dtype)

        on_edges(
            lambda: zero(first, depth, 0, W),
            lambda: zero(first + rows - depth, depth, 0, W),
            lambda: zero(first, rows, 0, 8),
            lambda: zero(first, rows, W - 8, 8),
        )

    clear_pad(2, 12, ((2, 12),))

    def shift_pool(r, carry):
        row = pad[r].astype(F32).reshape(W, C0)
        for b in range(3):
            xs[r, :, b * C0 : (b + 1) * C0] = ahead(row, b - 1).astype(BF16)
        return carry

    def gelu_row(r, carry):
        act1[r] = gelu_value(pre1[r])
        return carry

    def gelu_sides(r, carry):
        for col in (0, 64):
            act1[r, col : col + 16] = gelu_value(pre1[r, col : col + 16])
        return carry

    rows_loop(2, 14, shift_pool, 4)
    conv1_from([(2, 2, 0, W), (10, 2, 0, W)])
    rows_loop(2, 4, gelu_row, 2)
    rows_loop(10, 12, gelu_row, 2)
    conv1_from([(4, 6, 0, 16), (4, 6, 64, 16)])
    rows_loop(4, 10, gelu_sides, 6)
    clear_edges(act1, 2, 10, 1)

    def shift_first(r, carry):
        row = act1[r + 2]
        for b in range(3):
            fsm[r, :, b * C1 : (b + 1) * C1] = ahead(row, b - 1)[8:72].astype(BF16)
        return carry

    rows_loop(0, 10, shift_first, 5)

    def remote(source, target, send, recv, who):
        return pltpu.make_async_remote_copy(
            src_ref=source, dst_ref=target, send_sem=send, recv_sem=recv,
            device_id=who, device_id_type=MESH,
        )

    def by_core(who, act):
        pl.when(who == 0)(lambda: act(pl.ds(0, 384)))
        pl.when(who == 1)(lambda: act(pl.ds(0, 256)))

    def pair_piece(l, lanes):
        return remote(
            s0.at[l, 1 - core, :, :, lanes],
            r0.at[l, :, :, lanes],
            pair_send.at[l, 0],
            pair_recv.at[l, 0],
            partner,
        )

    def pair_mean(l):
        own = means.at[l, 2 * k + core]
        return remote(own, own, pair_send.at[l, 1], pair_recv.at[l, 1], partner)

    def pair_mean_in(l):
        other = means.at[l, 2 * k + 1 - core]
        return remote(other, other, pair_send.at[l, 1], pair_recv.at[l, 1], partner)

    def rs_piece(l, other, lanes):
        return remote(
            tsum.at[l, other, :, lanes], r1.at[l, k, :, lanes], rs_sem.at[l, 0, 0], rs_sem.at[l, 0, 1], xy_peer(other)
        )

    def rs_mean(l, other):
        both = means.at[l, pl.ds(2 * k, 2)]
        return remote(both, both, rs_sem.at[l, 1, 0], rs_sem.at[l, 1, 1], xy_peer(other))

    def z_piece(l, other, lanes):
        part = zb.at[l, z, :, lanes]
        return remote(part, part, z_sem.at[l, 0, 0], z_sem.at[l, 0, 1], z_peer(other))

    def z_mean(l, other):
        part = zm.at[l, z]
        return remote(part, part, z_sem.at[l, 1, 0], z_sem.at[l, 1, 1], z_peer(other))

    def ag_piece(l, n, lanes):
        part = ga.at[l, core, k, :, lanes]
        return remote(
            part, part, ag_send.at[l], ag_recv.at[l, n // 4], xy_peer(xy_others[n])
        )

    def fw_piece(l, slot, lanes):
        part = ga.at[l, core, slot, :, lanes]
        return remote(part, part, fw_sem.at[l, 0], fw_sem.at[l, 1], partner)

    def local_gram(l, values):
        mean = jnp.sum(values, axis=0, keepdims=True) * (1.0 / OWN)
        means[l, 2 * k + core] = mean
        cen = (values - mean).astype(BF16)
        pair_mean(l).start()
        gram = lax.dot_general(cen, cen, (((0,), (0,)), ((), ())), preferred_element_type=F32)
        for i in range(4):
            for d in range(3 if i < 2 else 2):
                j = (i + d) % 4
                block = gram[128 * i : 128 * i + 128, 128 * j : 128 * j + 128].astype(BF16)
                s0[l, i // 2, (i % 2) * 8 : (i % 2) * 8 + 8, :, 128 * d : 128 * d + 128] = (
                    block.reshape(8, 16, 128)
                )
        by_core(1 - core, lambda lanes: pair_piece(l, lanes).start())

    def rs_means(l):
        pair_mean_in(l).wait_recv()
        for other in xy_others:
            rs_mean(l, other).start()

    def rs_start(l):
        by_core(core, lambda lanes: wait_all(r0.at[l, :, :, lanes], pair_recv.at[l, 0]))
        tsum[l] = (s0[l, core].astype(F32) + r0[l].astype(F32)).astype(BF16)
        r1[l, k] = tsum[l, k]

        def send(lanes):
            for other in xy_others:
                rs_piece(l, other, lanes).start()

        by_core(core, send)

    def spread(rows):
        n = rows.shape[0]
        mean = jnp.sum(rows, axis=0, keepdims=True) * (1.0 / n)
        off = rows - mean
        dxs[0:n, 0:C1] = off
        dxs[0:n, C1:] = off[:, 0:256]
        lane = lax.broadcasted_iota(jnp.int32, (16, C1), 1)
        sub = lax.broadcasted_iota(jnp.int32, (16, C1), 0)
        pick = jnp.where(lane == strip * 16 + sub, 1.0, 0.0).astype(F32)
        left = lax.dot_general(
            pick, off, (((1,), (1,)), ((), ())), precision=HIGHEST, preferred_element_type=F32
        )
        right = dxs[0:n, pl.ds(pl.multiple_of((strip // 8) * 128, 128), 384)]
        return mean, jnp.dot(left, right, precision=HIGHEST, preferred_element_type=F32)

    def plane_done(l):
        wait_all(means.at[l, pl.ds(0, 30)], rs_sem.at[l, 1, 1])
        mean, extra = spread(means[l].reshape(32, C1))
        zm[l, z] = mean
        by_core(
            core,
            lambda lanes: wait_all(r1.at[l, pl.ds(0, 15), :, lanes], rs_sem.at[l, 0, 1]),
        )
        for other in z_others:
            z_mean(l, other).start()
        total = jnp.sum(r1[l].astype(F32), axis=0) + float(OWN) * extra
        zb[l, z] = total.astype(Z_TYPE)

        def send(lanes):
            for other in z_others:
                z_piece(l, other, lanes).start()

        by_core(core, send)

    def z_done(l):
        wait_all(zm.at[l, pl.ds(0, 7)], z_sem.at[l, 1, 1])
        mean, extra = spread(zm[l].reshape(8, C1))
        by_core(
            core, lambda lanes: wait_all(zb.at[l, pl.ds(0, 7), :, lanes], z_sem.at[l, 0, 1])
        )
        total = jnp.sum(zb[l].astype(F32), axis=0) + float(32 * OWN) * extra
        ga[l, core, k] = (total * (1.0 / CELLS)).astype(BF16)

        def send(lanes):
            for n in range(15):
                ag_piece(l, n, lanes).start()
            fw_piece(l, k, lanes).start()

        by_core(core, send)
        return mean

    def gathered(l):
        def forward(lanes):
            for n in range(15):
                if n % 4 == 0:
                    wait_all(
                        ga.at[l, core, pl.ds(0, min(4, 15 - n)), :, lanes], ag_recv.at[l, n // 4]
                    )
                fw_piece(l, xy_from[n], lanes).start()

        by_core(core, forward)

    def forwarded(l):
        by_core(1 - core, lambda lanes: wait_all(ga.at[l, 1 - core, :, :, lanes], fw_sem.at[l, 1]))

    def mismatch(l):
        def put(i, j, block):
            block = block - ts[l, 128 * i : 128 * i + 128, 128 * j : 128 * j + 128]
            top = block.astype(BF16)
            sh[l, 128 * i : 128 * i + 128, 128 * j : 128 * j + 128] = top
            sl[l, 128 * i : 128 * i + 128, 128 * j : 128 * j + 128] = (
                block - top.astype(F32)
            ).astype(BF16)

        for i in range(4):
            for d in range(3 if i < 2 else 2):
                block = ga[l, i // 2, (i % 2) * 8 : (i % 2) * 8 + 8, :, 128 * d : 128 * d + 128]
                block = block.astype(F32).reshape(128, 128)
                put(i, (i + d) % 4, block)
                if d > 0:
                    put((i + d) % 4, i, block.T)

    local_gram(0, flat(act1[3:11, 8:72, :]))

    loads[5].wait()

    def conv2_main(i, carry):
        total = None
        for a in range(3):
            part = dot_nn(flat(fsm[pl.ds(4 * i + a, 4)]), w2[a])
            total = part if total is None else total + part
        act2m[pl.ds(4 * i, 4)] = gelu_value(total).reshape(4, 64, C1)
        return carry

    conv2_main(0, 0)
    rs_means(0)
    rs_start(0)
    conv2_main(1, 0)
    local_gram(1, flat(act2m[...]))

    wait_all(pad.at[pl.ds(0, 5), pl.ds(0, 8)], halo_sem.at[2])
    clear_pad(0, 14, ((0, 2), (14, 2)))
    rows_loop(0, 2, shift_pool, 2)
    rows_loop(14, 16, shift_pool, 2)

    rs_means(1)
    conv1_from([(0, 2, 0, W), (12, 2, 0, W)])
    rs_start(1)

    def finish_first(r, carry):
        value, slope = gelu_both(pre1[r])
        act1[r] = value
        sl1[r] = slope
        return carry

    def shift_first_all(r, carry):
        row = act1[r]
        for b in range(3):
            fs[r, :, b * C1 : (b + 1) * C1] = ahead(row, b - 1).astype(BF16)
        return carry

    def conv2_all(i, carry):
        total = None
        for a in range(3):
            part = dot_nn(flat(fs[pl.ds(3 * i + a, 3)]), w2[a])
            total = part if total is None else total + part
        value, slope = gelu_both(total)
        act2[pl.ds(3 * i, 3)] = value.reshape(3, W, C1)
        sl2[pl.ds(3 * i, 3)] = slope.reshape(3, W, C1)
        return carry

    rows_loop(0, 14, finish_first, 2)
    clear_edges(act1, 0, 14, 3)
    clear_edges(sl1, 2, 10, 1)
    plane_done(0)
    rows_loop(0, 14, shift_first_all, 7)
    conv2_all(0, 0)
    plane_done(1)
    conv2_all(1, 0)
    mean_first = z_done(0)
    conv2_all(2, 0)
    mean_second = z_done(1)
    conv2_all(3, 0)
    clear_edges(sl2, 0, 12, 2)

    def centre(source, high, low, mean, shift):
        def step(r, carry):
            cen = source[r + shift] - mean
            top = cen.astype(BF16)
            high[r] = top
            low[r] = (cen - top.astype(F32)).astype(BF16)
            return carry

        return step

    rows_loop(0, 10, centre(act1, ch1, cl1, mean_first, 2), 5)
    rows_loop(0, 12, centre(act2, ch2, cl2, mean_second, 0), 4)

    def push(l, high, low, first, rows):
        top = flat(high[pl.ds(first, rows)])
        rest = flat(low[pl.ds(first, rows)])
        return dot_nn(top, sh[l]) + dot_nn(rest, sh[l]) + dot_nn(top, sl[l])

    def push_first(i, carry):
        flow1[pl.ds(5 * i, 5)] = push(0, ch1, cl1, 5 * i, 5).reshape(5, W, C1)
        return carry

    gathered(0)
    wait_all(pad.at[pl.ds(0, 12), pl.ds(0, 8)], halo_sem.at[0])
    for l in range(2):
        by_core(1 - core, lambda lanes: wait_all(r0.at[l, :, :, lanes], pair_send.at[l, 0]))
        pair_mean(l).wait_send()

        def sent(lanes):
            wait_all(r1.at[l, pl.ds(0, 15), :, lanes], rs_sem.at[l, 0, 0])
            wait_all(zb.at[l, pl.ds(0, 7), :, lanes], z_sem.at[l, 0, 0])

        by_core(core, sent)
        wait_all(means.at[l, pl.ds(0, 30)], rs_sem.at[l, 1, 0])
        wait_all(zm.at[l, pl.ds(0, 7)], z_sem.at[l, 1, 0])
    forwarded(0)
    mismatch(0)
    push_first(0, 0)
    gathered(1)
    push_first(1, 0)
    forwarded(1)

    mismatch(1)

    def back2(i, carry):
        grad = push(1, ch2, cl2, 4 * i, 4) * flat(sl2[pl.ds(4 * i, 4)])
        for b in range(3):
            gs2[pl.ds(4 * i, 4), :, b * C1 : (b + 1) * C1] = (
                ahead(grad, 1 - b).astype(BF16).reshape(4, W, C1)
            )
        return carry

    lax.fori_loop(0, 3, back2, 0, unroll=True)

    def back1(i, carry):
        flow = flat(flow1[pl.ds(5 * i, 5)])
        for a in range(3):
            for b in range(3):
                flow = flow + dot_nt(
                    flat(gs2[pl.ds(5 * i + 2 - a, 5), :, b * C1 : (b + 1) * C1]),
                    w2[a, b * C1 : (b + 1) * C1, :],
                )
        grad = flow * flat(sl1[pl.ds(5 * i + 2, 5)])
        for b in range(3):
            gs1[pl.ds(5 * i, 5), :, b * C1 : (b + 1) * C1] = (
                ahead(grad, 1 - b).reshape(5, W, C1)[:, 8:72].astype(BF16)
            )
        return carry

    lax.fori_loop(0, 2, back1, 0, unroll=True)

    for l in range(2):

        def gone(lanes):
            wait_all(ga.at[l, core, pl.ds(0, 15), :, lanes], ag_send.at[l])
            wait_all(ga.at[l, core, :, :, lanes], fw_sem.at[l, 0])

        by_core(core, gone)

    def back0(i, carry):
        total = None
        for a in range(3):
            for b in range(3):
                part = dot_nt(
                    flat(gs1[pl.ds(4 * i + 2 - a, 4), :, b * C1 : (b + 1) * C1]),
                    w1[a, b * C0 : (b + 1) * C0, :],
                )
                total = part if total is None else total + part
        out[pl.ds(4 * i, 4)] = total.reshape(4, 64, C0)
        return carry

    lax.fori_loop(0, 2, back0, 0, unroll=True)


def local(pool_input, weight_first, weight_second, targets):
    v = pltpu.VMEM
    dma = pltpu.SemaphoreType.DMA
    scratch = [
        v((8, 64, C0), F32),
        v((3, 3 * C0, C1), BF16),
        v((3, 3 * C1, C1), BF16),
        v((2, C1, C1), F32),
        v((2, C1, C1), F32),
        v((16, 10, 8, C0), BF16),
        v((16, W, 3 * C0), BF16),
        v((14, W, C1), F32),
        v((14, W, C1), F32),
        v((14, W, C1), F32),
        v((10, 64, 3 * C1), BF16),
        v((14, W, 3 * C1), BF16),
        v((8, 64, C1), F32),
        v((12, W, C1), F32),
        v((12, W, C1), F32),
        v((10, W, C1), BF16),
        v((10, W, C1), BF16),
        v((12, W, C1), BF16),
        v((12, W, C1), BF16),
        v((2, 2, 16, 16, 384), BF16),
        v((2, 16, 16, 384), BF16),
        v((2, 16, 16, 384), BF16),
        v((2, 16, 16, 384), BF16),
        v((2, 32, 1, C1), F32),
        v((32, C1 + 256), F32),
        v((2, 8, 16, 384), Z_TYPE),
        v((2, 8, 1, C1), F32),
        v((2, 2, 16, 16, 384), BF16),
        v((2, C1, C1), BF16),
        v((2, C1, C1), BF16),
        dma((6,)),
        dma((3,)),
        dma((2, 2)),
        dma((2, 2)),
        dma((2, 2, 2)),
        dma((2, 2, 2)),
        dma((2,)),
        dma((2, 4)),
        dma((2, 2)),
    ]
    return pl.pallas_call(
        kernel,
        out_shape=pltpu.VMEM((8, 64, C0), F32),
        in_specs=[pl.BlockSpec(memory_space=pltpu.HBM)] * 4,
        out_specs=pl.BlockSpec(memory_space=pltpu.VMEM),
        scratch_shapes=scratch,
        compiler_params=pltpu.CompilerParams(
            collective_id=0, has_side_effects=True, vmem_limit_bytes=67043328 - 768 * 1024
        ),
        name="style_grad",
    )(
        pool_input,
        weight_first.reshape(3, 3 * C0, C1),
        weight_second.reshape(3, 3 * C1, C1),
        targets,
    )


def solution(mesh):
    return jax.shard_map(
        local,
        mesh=mesh,
        in_specs=(P("grp", "tile", None), P(), P(), P()),
        out_specs=P("grp", "tile", None),
        check_vma=False,
    )
```
